32 devices in a mesh: dp: 8 (over z, y), seq: 4 (over x, core).
Axes of the slice: x: 2, y: 2, z: 4, core: 2. Of those that a mesh axis runs over, the one named last changes fastest.
Arguments:
- block_in: bfloat16 [8, 512, 1024], P('dp', 'seq'), may hold values from -6 to 6
- out_grad: bfloat16 [8, 512, 1024], P('dp', 'seq'), may hold values from -32 to 32
- gain_mix: float32 [1024], replicated, may hold values from 0.5 to 1.5
- w_query: bfloat16 [1024, 512], P('dp', 'seq')
- w_key: bfloat16 [1024, 128], P('dp', 'seq')
- w_value: bfloat16 [1024, 128], P('dp', 'seq'), may hold values from -0.1875 to 0.1875
- w_attn_out: bfloat16 [512, 1024], P('dp', 'seq'), may hold values from -1 to 1
- w_gate_z: bfloat16 [1024, 1536], P('dp', 'seq'), may hold values from -0.1875 to 0.1875
- w_ssm_x: bfloat16 [1024, 1536], P('dp', 'seq'), may hold values from -0.1875 to 0.1875
- w_ssm_bc: bfloat16 [1024, 256], P('dp', 'seq'), may hold values from -0.1875 to 0.1875
- w_ssm_dt: bfloat16 [1024, 24], P('dp', 'seq'), may hold values from -0.1875 to 0.1875
- conv_weight: float32 [4, 1792], replicated, may hold values from -3 to 3
- conv_bias: float32 [1792], replicated, may hold values from -3 to 3
- dt_bias: float32 [24], replicated, may hold values from -3 to 0
- a_log: float32 [24], replicated
- skip_d: float32 [24], replicated, may hold values from 0.5 to 1.5
- mamba_gain: float32 [1536], replicated, may hold values from 0.5 to 1.5
- w_mamba_out: bfloat16 [1536, 1024], P('dp', 'seq'), may hold values from -0.15625 to 0.15625
- gain_ffn: float32 [1024], replicated, may hold values from 0.5 to 1.5
- w_gate: bfloat16 [1024, 2048], P('dp', 'seq'), may hold values from -0.1875 to 0.1875
- w_up: bfloat16 [1024, 2048], P('dp', 'seq'), may hold values from -0.1875 to 0.1875
- w_down: bfloat16 [2048, 1024], P('dp', 'seq'), may hold values from -0.125 to 0.125
Outputs:
- block_out: bfloat16 [8, 512, 1024], P('dp', 'seq')
- input_grad: float32 [8, 512, 1024], P('dp', 'seq')
- grad_gain_mix: float32 [1024], replicated
- grad_query: float32 [1024, 512], P('dp', 'seq')
- grad_key: float32 [1024, 128], P('dp', 'seq')
- grad_value: float32 [1024, 128], P('dp', 'seq')
- grad_attn_out: float32 [512, 1024], P('dp', 'seq')
- grad_gate_z: float32 [1024, 1536], P('dp', 'seq')
- grad_ssm_x: float32 [1024, 1536], P('dp', 'seq')
- grad_ssm_bc: float32 [1024, 256], P('dp', 'seq')
- grad_ssm_dt: float32 [1024, 24], P('dp', 'seq')
- grad_conv_weight: float32 [4, 1792], replicated
- grad_conv_bias: float32 [1792], replicated
- grad_dt_bias: float32 [24], replicated
- grad_a_log: float32 [24], replicated
- grad_skip_d: float32 [24], replicated
- grad_mamba_gain: float32 [1536], replicated
- grad_mamba_out: float32 [1536, 1024], P('dp', 'seq')
- grad_gain_ffn: float32 [1024], replicated
- grad_gate: float32 [1024, 2048], P('dp', 'seq')
- grad_up: float32 [1024, 2048], P('dp', 'seq')
- grad_down: float32 [2048, 1024], P('dp', 'seq')
The draws below stay inside these ranges and needn't reach their ends.
All inputs are finite; a program needn't handle non-finite values.
Results may differ from the reference program's by a relative error of at most 0.017.
Values may be sent and summed in bfloat16 or wider, within the bound.
No kernel may reach another device: no remote copies, remote signals or barrier semaphores. Data moves between devices by JAX's collectives and lax.ppermute only.
A program may use at most 192 MiB of HBM per device.

```python
import math
import jax
import jax.numpy as jnp
from jax import lax

D = 1024
HQ = 8
HK = 2
HD = 64
HM = 24
PM = 64
NS = 128
FF = 2048
KC = 4
DI = 1536
LEN = 512
SEQS = 8


def attention_pair(key):
    key_base = jax.random.fold_in(key, 101)
    noise_key = jax.random.fold_in(key, 102)
    key_weight = jax.random.normal(key_base, (D, HK * HD), jnp.float32) * D ** (-0.5)
    noise = jax.random.normal(noise_key, (D, HQ * HD), jnp.float32) * D ** (-0.5)
    query_weight = noise
    return (query_weight, key_weight)


def draw_w_query(key, part):
    return attention_pair(key)[0].astype(jnp.bfloat16)


def draw_w_key(key, part):
    return attention_pair(key)[1].astype(jnp.bfloat16)


def draw_a_log(key, part):
    pick_key = jax.random.fold_in(key, 201)
    slow_key = jax.random.fold_in(key, 202)
    fast_key = jax.random.fold_in(key, 203)
    share = 0.5
    fast = jax.random.bernoulli(pick_key, share, (HM,))
    slow_rate = jnp.exp(jax.random.uniform(slow_key, (HM,), jnp.float32, math.log(0.3 / LEN), math.log(3.0 / LEN)))
    fast_rate = jnp.exp(jax.random.uniform(fast_key, (HM,), jnp.float32, math.log(0.05), math.log(0.3)))
    return jnp.log(jnp.where(fast, fast_rate, slow_rate)).astype(jnp.float32)


def draw_out_grad(key, part):
    base_key = jax.random.fold_in(key, 301)
    ramp = 1.0 + 2.0 * jnp.arange(SEQS, dtype=jnp.float32) / max(SEQS - 1, 1)
    ramp = ramp[:, None, None]
    values = jax.random.truncated_normal(base_key, -4.0, 4.0, (SEQS, LEN, D), jnp.float32) * ramp
    return values.astype(jnp.bfloat16)


def block_levels(key, dims, split, low, high):
    def one(axis_at, parts):
        steps = jax.random.uniform(jax.random.fold_in(jax.random.fold_in(key, 6), axis_at), (parts,), jnp.float32, low / len(split), high / len(split))
        return jnp.repeat(jnp.exp(steps), dims[axis_at] // parts).reshape((-1,) + (1,) * (len(dims) - axis_at - 1))

    level = one(*split[0])
    for cut in split[1:]:
        level = level * one(*cut)
    return level


def centred(own_key, extent, width, limit, shards=(), held_as=jnp.bfloat16):
    level = block_levels(own_key, extent, shards, -0.22, 0.18) if shards else 1.0
    array = jax.random.normal(own_key, extent, jnp.float32) * width * level
    return jnp.minimum(jnp.maximum(array, -limit), limit).astype(held_as)


def setup_inputs(seed: int = 0) -> dict:
    splits = jax.random.split(jax.random.key(seed), 23)
    return {
        "block_in": centred(splits[0], (SEQS, LEN, D), 1.0, 6.0, ((0, 8), (1, 4))),
        "out_grad": draw_out_grad(jax.random.fold_in(splits[22], 71), 0),
        "gain_mix": jnp.clip(1.0 + 0.1 * jax.random.normal(splits[2], (D,), jnp.float32), 0.5, 1.5),
        "w_query": draw_w_query(jax.random.fold_in(splits[22], 71), 0),
        "w_key": draw_w_key(jax.random.fold_in(splits[22], 71), 0),
        "w_value": centred(splits[5], (D, HK * HD), D ** -0.5, 0.1875, ((0, 8), (1, 4))),
        "w_attn_out": centred(splits[6], (HQ * HD, D), (HQ * HD // 16) ** -0.5, 1.0, ((0, 8), (1, 4))),
        "w_gate_z": centred(splits[7], (D, DI), D ** -0.5, 0.1875, ((0, 8), (1, 4))),
        "w_ssm_x": centred(splits[8], (D, DI), D ** -0.5, 0.1875, ((0, 8), (1, 4))),
        "w_ssm_bc": centred(splits[9], (D, 2 * NS), D ** -0.5, 0.1875, ((0, 8), (1, 4))),
        "w_ssm_dt": centred(splits[10], (D, HM), D ** -0.5, 0.1875, ((0, 8), (1, 4))),
        "conv_weight": centred(splits[11], (KC, DI + 2 * NS), 0.5, 3.0, (), jnp.float32),
        "conv_bias": centred(splits[12], (DI + 2 * NS,), 0.5, 3.0, (), jnp.float32),
        "dt_bias": jnp.clip(jax.random.uniform(splits[13], (HM,), jnp.float32, -3.0, 0.0), -3.0, 0.0),
        "a_log": draw_a_log(jax.random.fold_in(splits[22], 71), 0),
        "skip_d": jnp.clip(jax.random.uniform(splits[15], (HM,), jnp.float32, 0.5, 1.5), 0.5, 1.5),
        "mamba_gain": jnp.clip(1.0 + 0.1 * jax.random.normal(splits[16], (DI,), jnp.float32), 0.5, 1.5),
        "w_mamba_out": centred(splits[17], (DI, D), DI ** -0.5, 0.15625, ((0, 8), (1, 4))),
        "gain_ffn": jnp.clip(1.0 + 0.1 * jax.random.normal(splits[18], (D,), jnp.float32), 0.5, 1.5),
        "w_gate": centred(splits[19], (D, FF), D ** -0.5, 0.1875, ((0, 8), (1, 4))),
        "w_up": centred(splits[20], (D, FF), D ** -0.5, 0.1875, ((0, 8), (1, 4))),
        "w_down": centred(splits[21], (FF, D), FF ** -0.5, 0.125, ((0, 8), (1, 4))),
    }


norm_eps = 1e-05
highest = lax.Precision.HIGHEST

def rms_scale(values, gain):
    return values * lax.rsqrt(lax.optimization_barrier(jnp.mean(values * values, axis=-1, keepdims=True)) + norm_eps) * gain

def matmul(left, right):
    return jnp.dot(left, right, preferred_element_type=jnp.float32)

def inner_rows(left, right):
    return jnp.dot(left.T, right, preferred_element_type=jnp.float32)

def outer_cols(left, right):
    return jnp.dot(left, right.T, preferred_element_type=jnp.float32)

def conv_act(extended, conv_weight, conv_bias):
    row_count = extended.shape[0] - KC + 1
    total = conv_bias + conv_weight[0] * extended[0:row_count]
    for offset in range(1, KC):
        total = total + conv_weight[offset] * extended[offset:offset + row_count]
    return jax.nn.silu(total)

def ssd_block(state, pieces, a_rate):
    x_heads, dt_rows, b_rows, c_rows = pieces
    length = x_heads.shape[0]
    decay_cum = jnp.cumsum(dt_rows * a_rate, axis=0)
    rows_pos = lax.broadcasted_iota(jnp.int32, (length, length), 0)
    cols_pos = lax.broadcasted_iota(jnp.int32, (length, length), 1)
    causal = rows_pos >= cols_pos
    spread = decay_cum.T[:, :, None] - decay_cum.T[:, None, :]
    decay = jnp.where(causal, jnp.exp(jnp.where(causal, spread, 0.0)), 0.0)
    inner_cb = jnp.dot(c_rows, b_rows.T, precision=highest)
    mixing = decay * inner_cb[None] * dt_rows.T[:, None, :]
    y_inner = jnp.einsum('hts,shp->thp', mixing, x_heads, precision=highest)
    y_state = jnp.einsum('th,tn,hpn->thp', jnp.exp(decay_cum), c_rows, state, precision=highest)
    tail_decay = jnp.exp(decay_cum[-1][None, :] - decay_cum) * dt_rows
    new_state = jnp.exp(decay_cum[-1])[:, None, None] * state + jnp.einsum('sh,shp,sn->hpn', tail_decay, x_heads, b_rows, precision=highest)
    return (new_state, y_inner + y_state)

def ssd_run(x_heads, dt_rows, b_rows, c_rows, a_rate, state):
    total_rows = x_heads.shape[0]
    block = math.gcd(total_rows, 128)
    blocks = total_rows // block
    stacked = (x_heads.reshape(blocks, block, x_heads.shape[1], x_heads.shape[2]), dt_rows.reshape(blocks, block, dt_rows.shape[1]), b_rows.reshape(blocks, block, b_rows.shape[1]), c_rows.reshape(blocks, block, c_rows.shape[1]))
    final_state, outputs = lax.scan(lambda carry, piece: ssd_block(carry, piece, a_rate), state, stacked)
    return (outputs.reshape(total_rows, x_heads.shape[1], x_heads.shape[2]), final_state)

def mamba_tail(y_ssd, x_heads, gate_z, skip_d, mamba_gain):
    y_total = (y_ssd + skip_d[:, None] * x_heads).reshape(y_ssd.shape[0], -1)
    return rms_scale(y_total * jax.nn.silu(gate_z), mamba_gain)

def mamba_mid(extended, gate_z, dt_raw, conv_weight, conv_bias, dt_bias, a_log, skip_d, mamba_gain):
    act = conv_act(extended, conv_weight, conv_bias)
    row_count = act.shape[0]
    x_heads = act[:, :DI].reshape(row_count, HM, PM)
    b_rows = act[:, DI:DI + NS]
    c_rows = act[:, DI + NS:]
    dt_rows = jax.nn.softplus(dt_raw + dt_bias)
    a_rate = -jnp.exp(a_log)
    y_ssd, _ = ssd_run(x_heads, dt_rows, b_rows, c_rows, a_rate, jnp.zeros((HM, PM, NS), jnp.float32))
    return mamba_tail(y_ssd, x_heads, gate_z, skip_d, mamba_gain)

def attn_scores(queries, key_rows, q_start):
    q_count = queries.shape[0]
    k_count = key_rows.shape[0]
    q_heads = queries.astype(jnp.float32).reshape(q_count, HK, HQ // HK, HD)
    k_heads = key_rows.astype(jnp.float32).reshape(k_count, HK, HD)
    scores = jnp.einsum('tkgd,jkd->kgtj', q_heads, k_heads) * HD ** (-0.5)
    q_pos = q_start + lax.broadcasted_iota(jnp.int32, (q_count, k_count), 0)
    k_pos = lax.broadcasted_iota(jnp.int32, (q_count, k_count), 1)
    return jnp.where(k_pos <= q_pos, scores, -jnp.inf)

def attn_forward(queries, key_rows, value_rows, q_start):
    scores = attn_scores(queries, key_rows, q_start)
    top = lax.optimization_barrier(jnp.max(scores, axis=-1, keepdims=True))
    lse = top + jnp.log(lax.optimization_barrier(jnp.sum(jnp.exp(scores - top), axis=-1, keepdims=True)))
    probs = jnp.exp(scores - lse).astype(jnp.bfloat16)
    v_heads = value_rows.astype(jnp.float32).reshape(value_rows.shape[0], HK, HD)
    mixed = jnp.einsum('kgtj,jkd->tkgd', probs.astype(jnp.float32), v_heads)
    return (mixed.reshape(queries.shape[0], HQ * HD).astype(jnp.bfloat16), lse)

def attn_backward(queries, key_rows, value_rows, q_start, lse, grad_mix):
    q_count = queries.shape[0]
    k_count = key_rows.shape[0]
    scores = attn_scores(queries, key_rows, q_start)
    probs = jnp.exp(scores - lse)
    probs_b = probs.astype(jnp.bfloat16).astype(jnp.float32)
    grad_heads = grad_mix.astype(jnp.float32).reshape(q_count, HK, HQ // HK, HD)
    q_heads = queries.astype(jnp.float32).reshape(q_count, HK, HQ // HK, HD)
    k_heads = key_rows.astype(jnp.float32).reshape(k_count, HK, HD)
    v_heads = value_rows.astype(jnp.float32).reshape(k_count, HK, HD)
    d_values = jnp.einsum('kgtj,tkgd->jkd', probs_b, grad_heads)
    d_probs = jnp.einsum('tkgd,jkd->kgtj', grad_heads, v_heads)
    d_scores = probs * (d_probs - lax.optimization_barrier(jnp.sum(probs * d_probs, axis=-1, keepdims=True))) * HD ** (-0.5)
    d_scores = d_scores.astype(jnp.bfloat16).astype(jnp.float32)
    d_queries = jnp.einsum('kgtj,jkd->tkgd', d_scores, k_heads)
    d_keys = jnp.einsum('kgtj,tkgd->jkd', d_scores, q_heads)
    return (d_queries.reshape(q_count, HQ * HD), d_keys.reshape(k_count, HK * HD), d_values.reshape(k_count, HK * HD))

def reference(block_in, out_grad, gain_mix, w_query, w_key, w_value, w_attn_out, w_gate_z, w_ssm_x, w_ssm_bc, w_ssm_dt, conv_weight, conv_bias, dt_bias, a_log, skip_d, mamba_gain, w_mamba_out, gain_ffn, w_gate, w_up, w_down):
    params = (gain_mix, w_query, w_key, w_value, w_attn_out, w_gate_z, w_ssm_x, w_ssm_bc, w_ssm_dt, conv_weight, conv_bias, dt_bias, a_log, skip_d, mamba_gain, w_mamba_out, gain_ffn, w_gate, w_up, w_down)
    bf16 = jnp.bfloat16

    def one_sequence(totals, pieces):
        seq_in, seq_cot = pieces
        tokens = seq_in.astype(jnp.float32)
        normed_one, norm1_pull = jax.vjp(rms_scale, tokens, gain_mix)
        h1_b = normed_one.astype(bf16)
        queries = matmul(h1_b, w_query).astype(bf16)
        key_rows = matmul(h1_b, w_key).astype(bf16)
        value_rows = matmul(h1_b, w_value).astype(bf16)
        attn_mix, lse = attn_forward(queries, key_rows, value_rows, 0)
        attn_out = matmul(attn_mix, w_attn_out)
        gate_z = matmul(h1_b, w_gate_z)
        xbc = jnp.concatenate([matmul(h1_b, w_ssm_x), matmul(h1_b, w_ssm_bc)], axis=1)
        dt_raw = matmul(h1_b, w_ssm_dt)
        extended = jnp.concatenate([jnp.zeros((KC - 1, xbc.shape[1]), jnp.float32), xbc], axis=0)
        mamba_normed, mamba_pull = jax.vjp(mamba_mid, extended, gate_z, dt_raw, conv_weight, conv_bias, dt_bias, a_log, skip_d, mamba_gain)
        mamba_b = mamba_normed.astype(bf16)
        mamba_out = matmul(mamba_b, w_mamba_out)
        middle = tokens + attn_out + mamba_out
        normed_two, norm2_pull = jax.vjp(rms_scale, middle, gain_ffn)
        h2_b = normed_two.astype(bf16)
        gate_pre = matmul(h2_b, w_gate)
        up_pre = matmul(h2_b, w_up)
        hidden_b = (jax.nn.silu(gate_pre) * up_pre).astype(bf16)
        seq_out = (middle + matmul(hidden_b, w_down)).astype(bf16)
        d_out = seq_cot.astype(jnp.float32)
        g_down = inner_rows(hidden_b, seq_cot)
        d_hidden = outer_cols(seq_cot, w_down)
        sigma = jax.nn.sigmoid(gate_pre)
        d_gate = (d_hidden * up_pre * (sigma * (1.0 + gate_pre * (1.0 - sigma)))).astype(bf16)
        d_up = (d_hidden * gate_pre * sigma).astype(bf16)
        g_gate = inner_rows(h2_b, d_gate)
        g_up = inner_rows(h2_b, d_up)
        d_h2 = outer_cols(d_gate, w_gate) + outer_cols(d_up, w_up)
        d_mid_norm, g_gain_ffn = norm2_pull(d_h2)
        d_mid = d_out + d_mid_norm
        d_mid_b = d_mid.astype(bf16)
        g_attn_out = inner_rows(attn_mix, d_mid_b)
        g_mamba_out = inner_rows(mamba_b, d_mid_b)
        d_attn_mix = outer_cols(d_mid_b, w_attn_out).astype(bf16)
        d_mamba = outer_cols(d_mid_b, w_mamba_out)
        d_ext, d_gate_z, d_dt_raw, g_conv_w, g_conv_b, g_dt_bias, g_a_log, g_skip_d, g_mamba_gain = mamba_pull(d_mamba)
        d_xbc = d_ext[KC - 1:]
        d_queries, d_keys, d_values = attn_backward(queries, key_rows, value_rows, 0, lse, d_attn_mix)
        dq_b = d_queries.astype(bf16)
        dk_b = d_keys.astype(bf16)
        dv_b = d_values.astype(bf16)
        dz_b = d_gate_z.astype(bf16)
        dx_b = d_xbc[:, :DI].astype(bf16)
        dbc_b = d_xbc[:, DI:].astype(bf16)
        ddt_b = d_dt_raw.astype(bf16)
        d_h1 = outer_cols(dq_b, w_query) + outer_cols(dk_b, w_key) + outer_cols(dv_b, w_value)
        d_h1 = d_h1 + outer_cols(dz_b, w_gate_z) + outer_cols(dx_b, w_ssm_x) + outer_cols(dbc_b, w_ssm_bc) + outer_cols(ddt_b, w_ssm_dt)
        d_in_norm, g_gain_mix = norm1_pull(d_h1)
        seq_grad = d_mid + d_in_norm
        terms = (g_gain_mix, inner_rows(h1_b, dq_b), inner_rows(h1_b, dk_b), inner_rows(h1_b, dv_b), g_attn_out, inner_rows(h1_b, dz_b), inner_rows(h1_b, dx_b), inner_rows(h1_b, dbc_b), inner_rows(h1_b, ddt_b), g_conv_w, g_conv_b, g_dt_bias, g_a_log, g_skip_d, g_mamba_gain, g_mamba_out, g_gain_ffn, g_gate, g_up, g_down)
        new_totals = jax.tree.map(lambda total, term: total + term, totals, terms)
        return (new_totals, (seq_out, seq_grad))
    start = jax.tree.map(lambda param: jnp.zeros(param.shape, jnp.float32), params)
    totals, (outputs, in_grads) = lax.scan(one_sequence, start, (block_in, out_grad))
    return (outputs, in_grads, totals[0], totals[1], totals[2], totals[3], totals[4], totals[5], totals[6], totals[7], totals[8], totals[9], totals[10], totals[11], totals[12], totals[13], totals[14], totals[15], totals[16], totals[17], totals[18], totals[19])
```

```python
import jax
import jax.numpy as jnp
from jax import lax
from jax.sharding import PartitionSpec as P

HQ = 8
HK = 2
HD = 64
HM = 24
PM = 64
NS = 128
KC = 4
CHUNK = 128

f32 = jnp.float32
bf16 = jnp.bfloat16
norm_eps = 1e-05
highest = lax.Precision.HIGHEST


def exchange(block, axis, step):
    return lax.ppermute(block, axis, [(i, i ^ step) for i in range(lax.axis_size(axis))])


def steps_of(axis):
    count, step, steps = lax.axis_size(axis), 1, []
    while step < count:
        steps.append(step)
        step *= 2
    return steps


def bit_of(axis, step):
    return (lax.axis_index(axis) & step) != 0


def reorder(blocks, axis):
    for step in steps_of(axis):
        flag = bit_of(axis, step)
        blocks = [jnp.where(flag, blocks[i ^ step], blocks[i]) for i in range(len(blocks))]
    return blocks


def spread(block, axis):
    found = {0: block}
    for step in reversed(steps_of(axis)):
        for offset in sorted(found):
            found[offset ^ step] = exchange(found[offset], axis, step)
    return [found[i] for i in range(len(found))]


def gather_seq(block, dim):
    return jnp.concatenate(reorder(spread(block, "seq"), "seq"), axis=dim)


def split(array, dim):
    count = lax.axis_size("seq")
    width = array.shape[dim] // count
    return [lax.slice_in_dim(array, i * width, (i + 1) * width, axis=dim) for i in range(count)]


def reduce_seq(blocks):
    kept = dict(enumerate(reorder([b.astype(bf16) for b in blocks], "seq")))
    for step in steps_of("seq"):
        for offset in sorted(kept):
            if offset & step:
                got = exchange(kept.pop(offset), "seq", step)
                kept[offset ^ step] = kept[offset ^ step].astype(f32) + got.astype(f32)
        kept = {k: (v.astype(bf16) if len(kept) > 1 else v) for k, v in kept.items()}
    return kept[0]


def swap_seq(blocks):
    turned = reorder(blocks, "seq")
    got = [turned[0]] + [exchange(turned[j], "seq", j) for j in range(1, len(turned))]
    return reorder(got, "seq")


def sum_over(value, axes):
    for axis in axes:
        for step in steps_of(axis):
            value = value + exchange(value, axis, step)
    return value


def gather_dp(block):
    count, place = lax.axis_size("dp"), lax.axis_index("dp")
    parts = spread(block, "dp")
    whole = jnp.zeros((count,) + block.shape, block.dtype)
    for offset, part in enumerate(parts):
        whole = lax.dynamic_update_index_in_dim(whole, part, place ^ offset, 0)
    return whole


def reduce_dp(grad):
    count = lax.axis_size("dp")
    rows, cols = grad.shape
    held = grad.reshape(count, rows // count, cols)
    for step in steps_of("dp"):
        pairs = held.reshape(held.shape[0] // 2, 2, held.shape[1], cols)
        mine = bit_of("dp", step).astype(jnp.int32)
        away = lax.dynamic_index_in_dim(pairs, 1 - mine, 1, False).astype(bf16)
        stay = lax.dynamic_index_in_dim(pairs, mine, 1, False)
        held = stay.astype(f32) + exchange(away, "dp", step).astype(f32)
    return held[0]


def matmul(left, right):
    return jnp.dot(left, right, preferred_element_type=f32)


def inner_rows(left, right):
    return lax.dot_general(left, right, (((0,), (0,)), ((), ())), preferred_element_type=f32)


def outer_cols(left, right):
    return lax.dot_general(left, right, (((1,), (1,)), ((), ())), preferred_element_type=f32)


def rms_factor(values):
    return lax.rsqrt(jnp.mean(values * values, axis=-1, keepdims=True) + norm_eps)


def attn_scores(queries, keys, heads):
    count = queries.shape[0]
    scores = jnp.einsum("tgd,jd->gtj", queries, keys, preferred_element_type=f32) * HD ** (-0.5)
    rows_pos = lax.broadcasted_iota(jnp.int32, (count, count), 0)
    cols_pos = lax.broadcasted_iota(jnp.int32, (count, count), 1)
    return jnp.where(cols_pos <= rows_pos, scores, -jnp.inf)


def attn_forward(queries, keys, values):
    scores = attn_scores(queries, keys, queries.shape[1])
    top = jnp.max(scores, axis=-1, keepdims=True)
    lse = top + jnp.log(jnp.sum(jnp.exp(scores - top), axis=-1, keepdims=True))
    probs = jnp.exp(scores - lse).astype(bf16)
    mixed = jnp.einsum("gtj,jd->tgd", probs, values, preferred_element_type=f32)
    return mixed.reshape(mixed.shape[0], -1).astype(bf16), lse


def attn_backward(queries, keys, values, lse, grad_mix):
    probs = jnp.exp(attn_scores(queries, keys, queries.shape[1]) - lse)
    d_values = jnp.einsum("gtj,tgd->jd", probs.astype(bf16), grad_mix, preferred_element_type=f32)
    d_probs = jnp.einsum("tgd,jd->gtj", grad_mix, values, preferred_element_type=f32)
    d_scores = probs * (d_probs - jnp.sum(probs * d_probs, axis=-1, keepdims=True)) * HD ** (-0.5)
    d_scores = d_scores.astype(bf16)
    d_queries = jnp.einsum("gtj,jd->tgd", d_scores, keys, preferred_element_type=f32)
    d_keys = jnp.einsum("gtj,tgd->jd", d_scores, queries, preferred_element_type=f32)
    return d_queries.reshape(d_queries.shape[0], -1), d_keys, d_values


def product(spec, left, right):
    return jnp.einsum(spec, left, right, precision=ssd_precision)


ssd_precision = None


def conv_act(xbc, conv_weight, conv_bias):
    length = xbc.shape[0]
    extended = jnp.concatenate([jnp.zeros((KC - 1, xbc.shape[1]), f32), xbc], axis=0)
    total = conv_bias + conv_weight[0] * extended[0:length]
    for offset in range(1, KC):
        total = total + conv_weight[offset] * extended[offset : offset + length]
    return jax.nn.silu(total)


def mamba_local(xbc, gate_z, dt_raw, conv_weight, conv_bias, dt_bias, a_log, skip_d):
    length, inner = gate_z.shape
    heads = dt_raw.shape[1]
    chunk = CHUNK if length % CHUNK == 0 else length
    chunks = length // chunk
    act = conv_act(xbc, conv_weight, conv_bias)
    x_heads = act[:, :inner].reshape(chunks, chunk, heads, PM).transpose(0, 2, 1, 3)
    b_rows = act[:, inner : inner + NS].reshape(chunks, chunk, NS)
    c_rows = act[:, inner + NS :].reshape(chunks, chunk, NS)
    dt_rows = jax.nn.softplus(dt_raw + dt_bias)
    rate = -jnp.exp(a_log)
    dt_heads = dt_rows.reshape(chunks, chunk, heads).transpose(0, 2, 1)
    lower = lax.broadcasted_iota(jnp.int32, (chunk, chunk), 0) >= lax.broadcasted_iota(
        jnp.int32, (chunk, chunk), 1
    )
    steps = dt_heads * rate[None, :, None]
    cum = jnp.einsum("chs,ts->cht", steps, lower.astype(f32), precision=highest)
    spread_log = cum[:, :, :, None] - cum[:, :, None, :]
    decay = jnp.where(lower, jnp.exp(jnp.where(lower, spread_log, 0.0)), 0.0)
    inner_cb = product("ctn,csn->cts", c_rows, b_rows)
    mixing = decay * inner_cb[:, None] * dt_heads[:, :, None, :]
    y_inner = product("chts,chsp->chtp", mixing, x_heads)
    tail = jnp.exp(cum[:, :, -1:] - cum) * dt_heads
    gains = product("chsp,csn->chpn", x_heads * tail[..., None], b_rows)
    whole = jnp.exp(cum[:, :, -1])
    state, entering = jnp.zeros_like(gains[0]), []
    for k in range(chunks):
        entering.append(state)
        state = whole[k][:, None, None] * state + gains[k]
    entering = jnp.stack(entering)
    y_state = product("ctn,chpn->chtp", c_rows, entering) * jnp.exp(cum)[..., None]
    y_total = y_inner + y_state + skip_d[None, :, None, None] * x_heads
    y_total = y_total.transpose(0, 2, 1, 3).reshape(length, inner)
    return y_total * jax.nn.silu(gate_z)


def own_columns(array, width):
    return lax.dynamic_slice_in_dim(array, lax.axis_index("seq") * width, width, array.ndim - 1)


def placed(array, width):
    start = [0] * (array.ndim - 1) + [lax.axis_index("seq") * array.shape[-1]]
    return lax.dynamic_update_slice(
        jnp.zeros(array.shape[:-1] + (width,), array.dtype), array, start
    )


def per_device(
    block_in,
    out_grad,
    gain_mix,
    w_query,
    w_key,
    w_value,
    w_attn_out,
    w_gate_z,
    w_ssm_x,
    w_ssm_bc,
    w_ssm_dt,
    conv_weight,
    conv_bias,
    dt_bias,
    a_log,
    skip_d,
    mamba_gain,
    w_mamba_out,
    gain_ffn,
    w_gate,
    w_up,
    w_down,
):
    shards = lax.axis_size("seq")
    place = lax.axis_index("seq")
    groups = lax.axis_size("dp")
    model = block_in.shape[2]
    wide_q, wide_k, wide_bc = w_query.shape[1], w_key.shape[1], w_ssm_bc.shape[1]
    inner, heads, hidden_w = w_gate_z.shape[1], w_ssm_dt.shape[1], w_gate.shape[1]
    cols = w_attn_out.shape[1]
    kv_head = (place * (wide_q // HD)) // (HQ // HK)

    pack_in = jnp.concatenate(
        [w_query, w_gate_z, w_ssm_x, w_ssm_bc, w_key, w_value, w_ssm_dt], axis=1
    )
    token_blocks = spread(block_in[0], "seq")
    in_full = gather_dp(pack_in).reshape(model, -1)
    pack_out = jnp.concatenate([w_attn_out, w_mamba_out, w_down], axis=0)
    out_full = gather_dp(pack_out)
    pack_ffn = jnp.concatenate([w_gate, w_up], axis=1)
    ffn_full = gather_dp(pack_ffn).reshape(model, -1)
    rows_a, rows_m = w_attn_out.shape[0], w_mamba_out.shape[0]
    attn_out_full = out_full[:, :rows_a].reshape(-1, cols)
    mamba_out_full = out_full[:, rows_a : rows_a + rows_m].reshape(-1, cols)
    down_full = out_full[:, rows_a + rows_m :].reshape(-1, cols)

    tokens_b = jnp.concatenate(reorder(token_blocks, "seq"), axis=0)
    tokens = tokens_b.astype(f32)
    row_count = tokens.shape[0]
    local_rows = block_in.shape[1]
    scale_one = rms_factor(tokens)
    h1_b = (tokens * scale_one * gain_mix).astype(bf16)
    cuts = [wide_q, inner, inner, wide_bc + 2 * wide_k, heads]
    edges = [sum(cuts[:i]) for i in range(len(cuts) + 1)]
    shared = matmul(h1_b, in_full[:, edges[3] : edges[4]]).astype(bf16)
    shared_all = reorder(spread(shared, "seq"), "seq")
    queries = matmul(h1_b, in_full[:, : edges[1]]).astype(bf16).reshape(row_count, -1, HD)
    gate_z = matmul(h1_b, in_full[:, edges[1] : edges[2]])
    ssm_x = matmul(h1_b, in_full[:, edges[2] : edges[3]])
    dt_raw = matmul(h1_b, in_full[:, edges[4] :])
    xbc = jnp.concatenate([ssm_x] + [s[:, :wide_bc].astype(f32) for s in shared_all], axis=1)
    keys_all = jnp.concatenate([s[:, wide_bc : wide_bc + wide_k] for s in shared_all], axis=1)
    values_all = jnp.concatenate([s[:, wide_bc + wide_k :] for s in shared_all], axis=1)
    keys = lax.dynamic_slice_in_dim(keys_all, kv_head * HD, HD, 1)
    values = lax.dynamic_slice_in_dim(values_all, kv_head * HD, HD, 1)

    attn_local, lse = attn_forward(queries, keys, values)
    attn_mix = gather_seq(attn_local, 1)

    inner_all = inner * shards

    def own_conv(array):
        return jnp.concatenate(
            [own_columns(array[..., :inner_all], inner), array[..., inner_all:]], axis=-1
        )

    mixed_local, mamba_pull = jax.vjp(
        mamba_local,
        xbc,
        gate_z,
        dt_raw,
        own_conv(conv_weight),
        own_conv(conv_bias),
        own_columns(dt_bias, heads),
        own_columns(a_log, heads),
        own_columns(skip_d, heads),
    )
    mixed_b = gather_seq(mixed_local.astype(bf16), 1)
    mixed = mixed_b.astype(f32)
    scale_m = rms_factor(mixed)
    mamba_b = (mixed * scale_m * mamba_gain).astype(bf16)
    tokens_own = own_columns(tokens_b, cols).astype(f32)
    mamba_out = matmul(mamba_b, mamba_out_full)
    mid_own = tokens_own + matmul(attn_mix, attn_out_full) + mamba_out
    mid = gather_seq(mid_own.astype(bf16), 1).astype(f32)
    scale_two = rms_factor(mid)
    normed_two = mid * scale_two
    h2_b = (normed_two * gain_ffn).astype(bf16)
    both_pre = matmul(h2_b, ffn_full)
    gate_pre, up_pre = both_pre[:, :hidden_w], both_pre[:, hidden_w:]
    sigma = jax.nn.sigmoid(gate_pre)
    hidden_own = (gate_pre * sigma * up_pre).astype(bf16)

    cotangent = gather_seq(out_grad[0], 0)
    cot_own = own_columns(cotangent, cols)
    d_hidden = reduce_seq(split(outer_cols(cot_own, down_full), 1))
    d_gate = (d_hidden * up_pre * (sigma * (1.0 + gate_pre * (1.0 - sigma)))).astype(bf16)
    d_up = (d_hidden * gate_pre * sigma).astype(bf16)
    d_both = jnp.concatenate([d_gate, d_up], axis=1)
    d_h2 = outer_cols(d_both, ffn_full)
    along = sum_over(jnp.mean(d_h2 * gain_ffn * normed_two, axis=1), ("seq",))
    g_gain_ffn = jnp.sum(d_h2 * normed_two, axis=0)
    d_h2_own = reduce_seq(split(d_h2, 1))
    d_mid = cot_own.astype(f32) + scale_two * (
        d_h2_own * own_columns(gain_ffn, cols)
        - mid_own * scale_two * along[:, None]
    )
    d_mid_b = d_mid.astype(bf16)
    hidden_b = gather_seq(hidden_own, 1)
    block_own = (mid_own + matmul(hidden_b, down_full)).astype(bf16)
    block_out = jnp.concatenate(swap_seq(split_rows(block_own)), axis=1)
    g_ffn = reduce_dp(inner_rows(h2_b, d_both))
    g_down = reduce_dp(inner_rows(hidden_b, cot_own))

    d_normed = reduce_seq(split(outer_cols(d_mid_b, mamba_out_full), 1))
    along_m = sum_over(jnp.sum(d_mid_b.astype(f32) * mamba_out, axis=1), ("seq",)) / (
        inner_all
    )
    d_attn = reduce_seq(split(outer_cols(d_mid_b, attn_out_full), 1)).astype(bf16)
    mixed_own = own_columns(mixed_b, inner).astype(f32)
    gain_own = own_columns(mamba_gain, inner)
    normed_own = mixed_own * scale_m
    g_mamba_gain = jnp.sum(d_normed * normed_own, axis=0)
    d_mixed = scale_m * (d_normed * gain_own - normed_own * along_m[:, None])
    d_xbc, d_gate_z, d_dt_raw, g_conv_w, g_conv_b, g_dt_bias, g_a_log, g_skip = mamba_pull(d_mixed)
    g_attn_out = reduce_dp(inner_rows(attn_mix, d_mid_b))
    g_mamba_out = reduce_dp(inner_rows(mamba_b, d_mid_b))
    d_queries, d_keys, d_values = attn_backward(
        queries, keys, values, lse, d_attn.reshape(row_count, -1, HD)
    )

    def to_heads(part):
        blank = jnp.zeros((row_count, HK * HD), f32)
        return lax.dynamic_update_slice(blank, part, (0, kv_head * HD))

    bc_blocks = split(d_xbc[:, inner:], 1)
    k_blocks = split(to_heads(d_keys), 1)
    v_blocks = split(to_heads(d_values), 1)
    d_shared = reduce_seq(
        [jnp.concatenate(trio, axis=1) for trio in zip(bc_blocks, k_blocks, v_blocks)]
    )
    d_in = jnp.concatenate(
        [
            d_queries.astype(bf16),
            d_gate_z.astype(bf16),
            d_xbc[:, :inner].astype(bf16),
            d_shared.astype(bf16),
            d_dt_raw.astype(bf16),
        ],
        axis=1,
    )
    g_in = reduce_dp(inner_rows(h1_b, d_in))
    d_h1 = outer_cols(d_in, in_full)
    g_gain_mix = jnp.sum(d_h1 * (tokens * scale_one), axis=0)
    d_h1_own = reduce_seq(split(d_h1, 0))
    d_mid_rows = jnp.concatenate(swap_seq(split_rows(d_mid_b)), axis=1)
    x_own = block_in[0].astype(f32)
    scale_own = rms_factor(x_own)
    normed_x = x_own * scale_own
    d_norm = d_h1_own * gain_mix
    input_grad = d_mid_rows.astype(f32) + scale_own * (
        d_norm - normed_x * jnp.mean(d_norm * normed_x, axis=-1, keepdims=True)
    )

    def conv_whole(grad):
        return jnp.concatenate(
            [placed(grad[..., :inner], inner_all), grad[..., inner:]], axis=-1
        )

    small = [
        g_gain_mix,
        conv_whole(g_conv_w),
        conv_whole(g_conv_b),
        placed(g_dt_bias, HM),
        placed(g_a_log, HM),
        placed(g_skip, HM),
        placed(g_mamba_gain, inner_all),
        g_gain_ffn,
    ]
    sizes = [s.size for s in small]
    total = sum(sizes)
    flat = jnp.concatenate([s.reshape(-1) for s in small] + [jnp.zeros((-total % 1024,), f32)])
    flat = sum_over(flat.reshape(-1, 128), ("seq", "dp")).reshape(-1)
    starts = [sum(sizes[:i]) for i in range(len(sizes))]
    small = [flat[a : a + s.size].reshape(s.shape) for a, s in zip(starts, small)]

    at = [0, wide_q, wide_q + inner, wide_q + 2 * inner]
    at += [at[3] + wide_bc, at[3] + wide_bc + wide_k, at[3] + wide_bc + 2 * wide_k]
    return (
        block_out[None],
        input_grad[None],
        small[0],
        g_in[:, : at[1]],
        g_in[:, at[4] : at[5]],
        g_in[:, at[5] : at[6]],
        g_attn_out,
        g_in[:, at[1] : at[2]],
        g_in[:, at[2] : at[3]],
        g_in[:, at[3] : at[4]],
        g_in[:, at[6] :],
        small[1],
        small[2],
        small[3],
        small[4],
        small[5],
        small[6],
        g_mamba_out,
        small[7],
        g_ffn[:, :hidden_w],
        g_ffn[:, hidden_w:],
        g_down,
    )


def split_rows(array):
    return split(array, 0)


def solution(mesh):
    weight = P("dp", "seq")
    tokens = P("dp", "seq", None)
    args = (
        [tokens, tokens, P()]
        + [weight] * 8
        + [P()] * 6
        + [weight, P()]
        + [weight] * 3
    )
    outs = (
        [tokens, tokens, P()]
        + [weight] * 8
        + [P()] * 6
        + [weight, P()]
        + [weight] * 3
    )
    return jax.shard_map(
        per_device, mesh=mesh, in_specs=tuple(args), out_specs=tuple(outs), check_vma=False
    )
```

```python
import jax
import jax.numpy as jnp
from jax import lax
from jax.experimental import pallas as pl
from jax.experimental.pallas import tpu as pltpu
from jax.sharding import PartitionSpec as P

HQ = 8
HK = 2
HD = 64
HM = 24
PM = 64
NS = 128
KC = 4
CHUNK = 128

f32 = jnp.float32
bf16 = jnp.bfloat16
norm_eps = 1e-05
highest = lax.Precision.HIGHEST


def exchange(block, axis, step):
    return lax.ppermute(block, axis, [(i, i ^ step) for i in range(lax.axis_size(axis))])


def steps_of(axis):
    count, step, steps = lax.axis_size(axis), 1, []
    while step < count:
        steps.append(step)
        step *= 2
    return steps


def bit_of(axis, step):
    return (lax.axis_index(axis) & step) != 0


def reorder(blocks, axis):
    for step in steps_of(axis):
        flag = bit_of(axis, step)
        blocks = [jnp.where(flag, blocks[i ^ step], blocks[i]) for i in range(len(blocks))]
    return blocks


def spread(block, axis):
    found = {0: block}
    for step in reversed(steps_of(axis)):
        for offset in sorted(found):
            found[offset ^ step] = exchange(found[offset], axis, step)
    return [found[i] for i in range(len(found))]


def gather_seq(block, dim):
    return jnp.concatenate(reorder(spread(block, "seq"), "seq"), axis=dim)


def split(array, dim):
    count = lax.axis_size("seq")
    width = array.shape[dim] // count
    return [lax.slice_in_dim(array, i * width, (i + 1) * width, axis=dim) for i in range(count)]


def reduce_seq_parts(blocks):
    kept = dict(enumerate(reorder([b.astype(bf16) for b in blocks], "seq")))
    message = None
    for step in steps_of("seq"):
        for offset in sorted(kept):
            if offset & step:
                message = kept.pop(offset)
                got = exchange(message, "seq", step)
                kept[offset ^ step] = kept[offset ^ step].astype(f32) + got.astype(f32)
        kept = {k: (v.astype(bf16) if len(kept) > 1 else v) for k, v in kept.items()}
    return kept[0], message


def reduce_seq(blocks):
    return reduce_seq_parts(blocks)[0]


def swap_seq(blocks):
    blocks = reorder(blocks, "seq")
    for step in reversed(steps_of("seq")):
        moved = [j for j in range(len(blocks)) if j & step]
        got = exchange(jnp.stack([blocks[j] for j in moved]), "seq", step)
        for i, j in enumerate(moved):
            blocks[j] = got[i]
    return reorder(blocks, "seq")


def sum_over(value, axes):
    for axis in axes:
        for step in steps_of(axis):
            value = value + exchange(value, axis, step)
    return value


def gather_dp(block):
    count, place = lax.axis_size("dp"), lax.axis_index("dp")
    parts = spread(block, "dp")
    whole = jnp.zeros((count,) + block.shape, block.dtype)
    for offset, part in enumerate(parts):
        whole = lax.dynamic_update_index_in_dim(whole, part, place ^ offset, 0)
    return whole


def after(value, gate):
    return value if gate is None else lax.optimization_barrier((value, gate))[0]


class Reduction:
    def __init__(self, grad):
        count = lax.axis_size("dp")
        self.left = steps_of("dp")
        self.send(grad.reshape(count, grad.shape[0] // count, grad.shape[1]))

    def send(self, held):
        step = self.left.pop(0)
        mine = bit_of("dp", step).astype(jnp.int32)
        pairs = held.reshape(held.shape[0] // 2, 2, held.shape[1], held.shape[2])
        self.message = lax.dynamic_index_in_dim(pairs, 1 - mine, 1, False).astype(bf16)
        self.stay = lax.dynamic_index_in_dim(pairs, mine, 1, False).astype(f32)
        self.got = exchange(self.message, "dp", step)

    def advance(self, gate=None):
        if self.left:
            self.send(self.stay + after(self.got, gate).astype(f32))
        return self.message

    def finish(self, cuts):
        while self.left:
            self.advance()
        return [self.stay[0][:, c] + self.got[0][:, c].astype(f32) for c in cuts]


def matmul(left, right):
    return jnp.dot(left, right, preferred_element_type=f32)


def inner_rows(left, right):
    return lax.dot_general(left, right, (((0,), (0,)), ((), ())), preferred_element_type=f32)


def outer_cols(left, right):
    return lax.dot_general(left, right, (((1,), (1,)), ((), ())), preferred_element_type=f32)


def rms_factor(values):
    return lax.rsqrt(jnp.mean(values * values, axis=-1, keepdims=True) + norm_eps)


def masked_scores(q_ref, k_ref, at, first, count):
    scores = dot(q_ref[first : first + count, at], k_ref[0 : first + count, :], (1, 1)) * HD ** (-0.5)
    rows = lax.broadcasted_iota(jnp.int32, scores.shape, 0) + first
    cols = lax.broadcasted_iota(jnp.int32, scores.shape, 1)
    return jnp.where(cols <= rows, scores, -jnp.inf)


def attn_fwd_kernel(q_ref, k_ref, v_ref, mix_ref, lse_ref):
    length, width = q_ref.shape
    count = CHUNK if length % CHUNK == 0 else length
    for h in range(width // HD):
        at = slice(h * HD, (h + 1) * HD)
        for first in range(0, length, count):
            scores = masked_scores(q_ref, k_ref, at, first, count)
            top = jnp.max(scores, axis=1, keepdims=True)
            lse = top + jnp.log(jnp.sum(jnp.exp(scores - top), axis=1, keepdims=True))
            probs = jnp.exp(scores - lse).astype(bf16)
            here = slice(first, first + count)
            mix_ref[here, at] = dot(probs, v_ref[0 : first + count, :]).astype(bf16)
            lse_ref[here, h : h + 1] = lse


def attn_bwd_kernel(q_ref, k_ref, v_ref, lse_ref, grad_ref, dq_ref, dk_ref, dv_ref):
    length, width = q_ref.shape
    count = CHUNK if length % CHUNK == 0 else length
    dk_ref[...] = jnp.zeros_like(dk_ref)
    dv_ref[...] = jnp.zeros_like(dv_ref)
    for h in range(width // HD):
        at = slice(h * HD, (h + 1) * HD)
        for first in range(0, length, count):
            here, until = slice(first, first + count), slice(0, first + count)
            grad = grad_ref[here, at]
            probs = jnp.exp(masked_scores(q_ref, k_ref, at, first, count) - lse_ref[here, h : h + 1])
            dv_ref[until, :] = dv_ref[until, :] + dot(probs.astype(bf16), grad, (0, 0))
            d_probs = dot(grad, v_ref[until, :], (1, 1))
            inner = jnp.sum(probs * d_probs, axis=1, keepdims=True)
            d_scores = (probs * (d_probs - inner) * HD ** (-0.5)).astype(bf16)
            dq_ref[here, at] = dot(d_scores, k_ref[until, :]).astype(bf16)
            dk_ref[until, :] = dk_ref[until, :] + dot(d_scores, q_ref[here, at], (0, 0))


def input_grad_kernel(d_ref, w_ref, x_ref, scale_ref, out_ref, gain_ref):
    @pl.when(pl.program_id(0) == 0)
    def _():
        gain_ref[...] = jnp.zeros_like(gain_ref)

    grad = dot(d_ref[...], w_ref[...], (1, 1))
    out_ref[...] = grad.astype(bf16)
    normed = x_ref[...].astype(f32) * scale_ref[...]
    gain_ref[...] = gain_ref[...] + jnp.sum(grad * normed, axis=0, keepdims=True)


def input_grad_parts(d_in, weights, tokens, scale, blocks):
    length, width = d_in.shape
    model = weights.shape[0]
    count = length // blocks
    rows = lambda w: pl.BlockSpec((count, w), lambda i: (i, 0))
    grads, gain = pl.pallas_call(
        input_grad_kernel,
        grid=(blocks,),
        in_specs=[rows(width), full_spec(weights.shape), rows(model), rows(1)],
        out_specs=[rows(model), full_spec((1, model))],
        out_shape=[
            jax.ShapeDtypeStruct((length, model), bf16),
            jax.ShapeDtypeStruct((1, model), f32),
        ],
        name="input_grad",
    )(d_in, weights, tokens, scale)
    return grads, gain[0]


def attn_forward(queries, keys, values):
    length, width = queries.shape
    return pl.pallas_call(
        attn_fwd_kernel,
        out_shape=[
            jax.ShapeDtypeStruct((length, width), bf16),
            jax.ShapeDtypeStruct((length, 128), f32),
        ],
        name="attn_fwd",
    )(queries, keys, values)


def attn_backward(queries, keys, values, lse, grad_mix):
    return pl.pallas_call(
        attn_bwd_kernel,
        out_shape=[
            jax.ShapeDtypeStruct(queries.shape, bf16),
            jax.ShapeDtypeStruct(keys.shape, f32),
            jax.ShapeDtypeStruct(values.shape, f32),
        ],
        name="attn_bwd",
    )(queries, keys, values, lse, grad_mix)


def dot(left, right, over=(1, 0), precision=None):
    return lax.dot_general(
        left,
        right,
        (((over[0],), (over[1],)), ((), ())),
        precision=precision,
        preferred_element_type=f32,
    )


def head_map(lanes, inner):
    rows = lax.broadcasted_iota(jnp.int32, (lanes, inner), 0) * PM
    cols = lax.broadcasted_iota(jnp.int32, (lanes, inner), 1)
    return ((cols >= rows) & (cols < rows + PM)).astype(f32)


def chunk_terms(dt_in, log_rate, inner):
    count, lanes = dt_in.shape
    rows = lax.broadcasted_iota(jnp.int32, (count, count), 0)
    cols = lax.broadcasted_iota(jnp.int32, (count, count), 1)
    lower = rows >= cols
    dt = jax.nn.softplus(dt_in)
    rate = -jnp.exp(log_rate)
    cum = dot(lower.astype(f32), dt * rate, precision=highest)
    rest = jnp.exp(cum[count - 1 :, :] - cum)
    spread_map = head_map(lanes, inner)
    grown = dot(jnp.exp(cum), spread_map, precision=highest)
    tail = dot(rest * dt, spread_map, precision=highest)
    return lower, dt, rate, cum, rest, spread_map, grown, tail


def mamba_fwd_kernel(
    x_ref, bc_ref, z_ref, dt_ref, w_ref, bias_ref, head_ref, skip_ref,
    u_ref, y_ref, total_ref, state_ref, ext, state,
):
    count, inner = x_ref.shape

    @pl.when(pl.program_id(0) == 0)
    def _():
        state[...] = jnp.zeros_like(state)
        ext[...] = jnp.zeros_like(ext)

    ext[0:8, :] = ext[count : count + 8, :]
    ext[8 : 8 + count, :inner] = x_ref[...]
    ext[8 : 8 + count, inner:] = bc_ref[...].astype(f32)
    total = bias_ref[...] + w_ref[0:1, :] * ext[8 - KC + 1 : 8 - KC + 1 + count, :]
    for k in range(1, KC):
        total = total + w_ref[k : k + 1, :] * ext[8 - KC + 1 + k : 8 - KC + 1 + k + count, :]
    total_ref[...] = total
    act = total * jax.nn.sigmoid(total)
    x, b_rows, c_rows = act[:, :inner], act[:, inner : inner + NS], act[:, inner + NS :]
    lower, dt, rate, cum, rest, spread_map, grown, tail = chunk_terms(
        dt_ref[...] + head_ref[0:1, :], head_ref[1:2, :], inner
    )
    cum_t, dt_t = cum.T, dt.T
    x_b, b_b, c_b = x.astype(bf16), b_rows.astype(bf16), c_rows.astype(bf16)
    entering = state[...]
    state_ref[0] = entering
    between = dot(c_b, b_b, (1, 1))
    y_ref[...] = dot(c_b, entering.astype(bf16)) * grown + skip_ref[...] * x
    for h in range(inner // PM):
        at = slice(h * PM, (h + 1) * PM)
        gap = jnp.where(lower, cum[:, h : h + 1] - cum_t[h : h + 1, :], 0.0)
        mix = jnp.where(lower, jnp.exp(gap) * between * dt_t[h : h + 1, :], 0.0)
        y_ref[:, at] = y_ref[:, at] + dot(mix.astype(bf16), x_b[:, at])
    state[...] = entering * grown[count - 1 :, :] + dot(b_b, (x * tail).astype(bf16), (0, 0))
    z = z_ref[...]
    u_ref[...] = (y_ref[...] * (z * jax.nn.sigmoid(z))).astype(bf16)


def mamba_bwd_kernel(
    dy_ref, total_ref, x_ref, bc_ref, dt_ref, state_ref, w_ref, head_ref, skip_ref,
    dx_ref, dbc_ref, ddt_ref, gconv_ref, ghead_ref, ext, carry, rows_ref, dact,
):
    count, inner = x_ref.shape
    lanes = dt_ref.shape[1]

    @pl.when(pl.program_id(0) == 0)
    def _():
        carry[...] = jnp.zeros_like(carry)
        ext[...] = jnp.zeros_like(ext)
        rows_ref[...] = jnp.zeros_like(rows_ref)
        gconv_ref[...] = jnp.zeros_like(gconv_ref)
        ghead_ref[...] = jnp.zeros_like(ghead_ref)

    total = total_ref[...]
    gate = jax.nn.sigmoid(total)
    act = total * gate
    x, b_rows, c_rows = act[:, :inner], act[:, inner : inner + NS], act[:, inner + NS :]
    dy = dy_ref[...]
    skipped = jnp.sum(dy * x, axis=0, keepdims=True)
    dt_in = dt_ref[...] + head_ref[0:1, :]
    lower, dt, rate, cum, rest, spread_map, grown, tail = chunk_terms(
        dt_in, head_ref[1:2, :], inner
    )
    cum_t, dt_t = cum.T, dt.T
    x_b, b_b, c_b, dy_b = x.astype(bf16), b_rows.astype(bf16), c_rows.astype(bf16), dy.astype(bf16)
    entering, leaving = state_ref[0], carry[...]
    entering_b, leaving_b = entering.astype(bf16), leaving.astype(bf16)
    last = grown[count - 1 :, :]
    dye_b = (dy * grown).astype(bf16)
    y_state = dot(c_b, entering_b) * grown
    d_xw = dot(b_b, leaving_b)
    d_b = dot((x * tail).astype(bf16), leaving_b, (1, 1))
    d_c = dot(dye_b, entering_b, (1, 1))
    carry[...] = leaving * last + dot(c_b, dye_b, (0, 0))
    d_cum = dot(dy * y_state, spread_map, (1, 1), highest)
    d_tail = dot(d_xw * x, spread_map, (1, 1), highest)
    d_last = dot(
        jnp.sum(leaving * entering, axis=0, keepdims=True) * last, spread_map, (1, 1), highest
    )
    dact[:, :inner] = skip_ref[...] * dy + d_xw * tail
    between = dot(c_b, b_b, (1, 1))
    d_between = jnp.zeros_like(between)
    lane = lax.broadcasted_iota(jnp.int32, (count, lanes), 1)
    for h in range(inner // PM):
        at = slice(h * PM, (h + 1) * PM)
        gap = jnp.where(lower, cum[:, h : h + 1] - cum_t[h : h + 1, :], 0.0)
        decay = jnp.where(lower, jnp.exp(gap), 0.0)
        d_mix = dot(dy_b[:, at], x_b[:, at], (1, 1)) * decay
        d_between = d_between + d_mix * dt_t[h : h + 1, :]
        part = d_mix * between
        rows_ref[h : h + 1, :] = jnp.sum(part, axis=0, keepdims=True)
        along = jnp.sum(part * dt_t[h : h + 1, :], axis=1, keepdims=True)
        d_cum = d_cum + jnp.where(lane == h, along, 0.0)
        mix = (decay * between * dt_t[h : h + 1, :]).astype(bf16)
        dact[:, at] = dact[:, at] + dot(mix, dy_b[:, at], (0, 0))
    d_between_b = d_between.astype(bf16)
    d_c = d_c + dot(d_between_b, b_b)
    d_b = d_b + dot(d_between_b, c_b, (0, 0))
    dact[:, inner : inner + NS] = d_b
    dact[:, inner + NS :] = d_c
    d_dt = rows_ref[...].T
    d_decay = d_tail * rest * dt
    d_cum = d_cum - d_decay - dt * d_dt
    d_last = d_last + jnp.sum(d_decay, axis=0, keepdims=True)
    d_step = dot(lower.astype(f32), d_cum, (0, 0), highest) + d_last
    d_dt = d_dt + d_tail * rest + d_step * rate
    d_raw = d_dt * jax.nn.sigmoid(dt_in)
    ddt_ref[...] = d_raw.astype(bf16)
    ghead_ref[0:1, :] = ghead_ref[0:1, :] + jnp.sum(d_raw, axis=0, keepdims=True)
    ghead_ref[1:2, :] = ghead_ref[1:2, :] + jnp.sum(d_step * dt, axis=0, keepdims=True) * rate
    ghead_ref[2:3, :] = ghead_ref[2:3, :] + dot(skipped, spread_map, (1, 1), highest)
    d_total = dact[...] * (gate * (1.0 + total * (1.0 - gate)))
    ext[count : count + 8, :] = ext[0:8, :]
    ext[0:count, :] = d_total
    gconv_ref[KC : KC + 1, :] = gconv_ref[KC : KC + 1, :] + jnp.sum(d_total, axis=0, keepdims=True)
    d_x, d_bc = jnp.zeros_like(x), jnp.zeros((count, 2 * NS), f32)
    x_in, bc_in = x_ref[...], bc_ref[...].astype(f32)
    for k in range(KC):
        moved = ext[KC - 1 - k : KC - 1 - k + count, :]
        d_x = d_x + w_ref[k : k + 1, :inner] * moved[:, :inner]
        d_bc = d_bc + w_ref[k : k + 1, inner:] * moved[:, inner:]
        gconv_ref[k : k + 1, :inner] = gconv_ref[k : k + 1, :inner] + jnp.sum(
            x_in * moved[:, :inner], axis=0, keepdims=True
        )
        gconv_ref[k : k + 1, inner:] = gconv_ref[k : k + 1, inner:] + jnp.sum(
            bc_in * moved[:, inner:], axis=0, keepdims=True
        )
    dx_ref[...] = d_x.astype(bf16)
    dbc_ref[...] = d_bc


def rows_spec(width, chunk, chunks, back):
    return pl.BlockSpec((chunk, width), lambda c: (chunks - 1 - c if back else c, 0))


def full_spec(shape):
    return pl.BlockSpec(shape, lambda c: (0,) * len(shape))


def mamba_forward(x_pre, bc_pre, gate_z, dt_raw, conv_w, head_rows, skip_row, conv_b):
    length, inner = x_pre.shape
    chunk = CHUNK if length % CHUNK == 0 else length
    chunks = length // chunk
    wide = inner + 2 * NS
    rows = lambda width: rows_spec(width, chunk, chunks, False)
    return pl.pallas_call(
        mamba_fwd_kernel,
        grid=(chunks,),
        in_specs=[
            rows(inner), rows(2 * NS), rows(inner), rows(dt_raw.shape[1]),
            full_spec(conv_w.shape), full_spec(conv_b.shape), full_spec(head_rows.shape),
            full_spec(skip_row.shape),
        ],
        out_specs=[
            rows(inner), rows(inner), rows(wide),
            pl.BlockSpec((1, NS, inner), lambda c: (c, 0, 0)),
        ],
        out_shape=[
            jax.ShapeDtypeStruct((length, inner), bf16),
            jax.ShapeDtypeStruct((length, inner), f32),
            jax.ShapeDtypeStruct((length, wide), f32),
            jax.ShapeDtypeStruct((chunks, NS, inner), f32),
        ],
        scratch_shapes=[pltpu.VMEM((chunk + 8, wide), f32), pltpu.VMEM((NS, inner), f32)],
        name="mamba_fwd",
    )(x_pre, bc_pre, gate_z, dt_raw, conv_w, conv_b, head_rows, skip_row)


def mamba_backward(
    d_y, total, x_pre, bc_pre, dt_raw, states, conv_w, head_rows, skip_row
):
    length, inner = x_pre.shape
    chunks = states.shape[0]
    chunk = length // chunks
    wide, lanes = inner + 2 * NS, dt_raw.shape[1]
    rows = lambda width: rows_spec(width, chunk, chunks, True)
    return pl.pallas_call(
        mamba_bwd_kernel,
        grid=(chunks,),
        in_specs=[
            rows(inner), rows(wide), rows(inner), rows(2 * NS), rows(lanes),
            pl.BlockSpec((1, NS, inner), lambda c: (chunks - 1 - c, 0, 0)),
            full_spec(conv_w.shape), full_spec(head_rows.shape), full_spec(skip_row.shape),
        ],
        out_specs=[
            rows(inner), rows(2 * NS), rows(lanes),
            full_spec((8, wide)), full_spec((8, lanes)),
        ],
        out_shape=[
            jax.ShapeDtypeStruct((length, inner), bf16),
            jax.ShapeDtypeStruct((length, 2 * NS), f32),
            jax.ShapeDtypeStruct((length, lanes), bf16),
            jax.ShapeDtypeStruct((8, wide), f32),
            jax.ShapeDtypeStruct((8, lanes), f32),
        ],
        scratch_shapes=[
            pltpu.VMEM((chunk + 8, wide), f32),
            pltpu.VMEM((NS, inner), f32),
            pltpu.VMEM((lanes, chunk), f32),
            pltpu.VMEM((chunk, wide), f32),
        ],
        name="mamba_bwd",
    )(d_y, total, x_pre, bc_pre, dt_raw, states, conv_w, head_rows, skip_row)


def own_columns(array, width):
    return lax.dynamic_slice_in_dim(array, lax.axis_index("seq") * width, width, array.ndim - 1)


def placed(array, width):
    start = [0] * (array.ndim - 1) + [lax.axis_index("seq") * array.shape[-1]]
    return lax.dynamic_update_slice(
        jnp.zeros(array.shape[:-1] + (width,), array.dtype), array, start
    )


def per_device(
    block_in,
    out_grad,
    gain_mix,
    w_query,
    w_key,
    w_value,
    w_attn_out,
    w_gate_z,
    w_ssm_x,
    w_ssm_bc,
    w_ssm_dt,
    conv_weight,
    conv_bias,
    dt_bias,
    a_log,
    skip_d,
    mamba_gain,
    w_mamba_out,
    gain_ffn,
    w_gate,
    w_up,
    w_down,
):
    shards = lax.axis_size("seq")
    place = lax.axis_index("seq")
    groups = lax.axis_size("dp")
    model = block_in.shape[2]
    wide_q, wide_k, wide_bc = w_query.shape[1], w_key.shape[1], w_ssm_bc.shape[1]
    inner, heads, hidden_w = w_gate_z.shape[1], w_ssm_dt.shape[1], w_gate.shape[1]
    cols = w_attn_out.shape[1]
    kv_head = (place * (wide_q // HD)) // (HQ // HK)

    lanes = 128
    fill = -heads % lanes
    pack_in = jnp.concatenate(
        [w_query, w_gate_z, w_ssm_x, jnp.pad(w_ssm_dt, ((0, 0), (0, fill))), w_ssm_bc, w_key, w_value],
        axis=1,
    )
    in_full = gather_dp(pack_in).reshape(model, -1)
    out_grad_b, block_in_b = out_grad[0], block_in[0]
    token_blocks = spread(jnp.concatenate([block_in_b, out_grad_b], axis=1), "seq")
    rows_a, rows_m = w_attn_out.shape[0], w_mamba_out.shape[0]
    pack_out = jnp.concatenate([w_attn_out, w_mamba_out, w_down], axis=0)
    rows_w = w_gate.shape[0]
    stacks = pack_out.shape[0] // rows_w
    pack_rest = jnp.concatenate(
        [w_gate, w_up] + [pack_out[i * rows_w : (i + 1) * rows_w] for i in range(stacks)], axis=1
    )
    rest_full = lax.all_gather(pack_rest, "dp", axis=0)
    ffn_full = rest_full[:, :, : 2 * hidden_w].reshape(model, 2 * hidden_w)
    out_full = jnp.concatenate(
        [
            rest_full[:, :, 2 * hidden_w + i * cols : 2 * hidden_w + (i + 1) * cols]
            for i in range(stacks)
        ],
        axis=1,
    )
    attn_out_full = out_full[:, :rows_a].reshape(-1, cols)
    mamba_out_full = out_full[:, rows_a : rows_a + rows_m].reshape(-1, cols)
    down_full = out_full[:, rows_a + rows_m :].reshape(-1, cols)

    both = jnp.concatenate(reorder(token_blocks, "seq"), axis=0)
    tokens_b, cotangent = both[:, :model], both[:, model:]
    tokens = tokens_b.astype(f32)
    row_count = tokens.shape[0]
    local_rows = block_in.shape[1]
    scale_one = rms_factor(tokens)
    h1_b = (tokens * scale_one * gain_mix).astype(bf16)
    cuts = [wide_q, inner, inner, heads + fill, wide_bc + 2 * wide_k]
    edges = [sum(cuts[:i]) for i in range(len(cuts) + 1)]
    shared = matmul(h1_b, in_full[:, edges[4] :]).astype(bf16)
    shared_all = reorder(spread(shared, "seq"), "seq")
    queries = matmul(h1_b, in_full[:, : edges[1]]).astype(bf16)
    gate_z = matmul(h1_b, in_full[:, edges[1] : edges[2]])
    ssm_x = matmul(h1_b, in_full[:, edges[2] : edges[3]])
    dt_raw = matmul(h1_b, in_full[:, edges[3] : edges[4]])
    bc_pre = jnp.concatenate([s[:, :wide_bc] for s in shared_all], axis=1)
    keys_all = jnp.concatenate([s[:, wide_bc : wide_bc + wide_k] for s in shared_all], axis=1)
    values_all = jnp.concatenate([s[:, wide_bc + wide_k :] for s in shared_all], axis=1)
    keys = lax.dynamic_slice_in_dim(keys_all, kv_head * HD, HD, 1)
    values = lax.dynamic_slice_in_dim(values_all, kv_head * HD, HD, 1)

    attn_local, lse = attn_forward(queries, keys, values)
    attn_mix = gather_seq(attn_local, 1)

    inner_all = inner * shards

    def own_conv(array):
        return jnp.concatenate(
            [own_columns(array[..., :inner_all], inner), array[..., inner_all:]], axis=-1
        )

    conv_w, conv_b = own_conv(conv_weight), own_conv(conv_bias)[None]
    head_rows = jnp.pad(
        jnp.stack([own_columns(dt_bias, heads), own_columns(a_log, heads)]), ((0, 0), (0, fill))
    )
    skip_row = jnp.repeat(own_columns(skip_d, heads), inner // heads)[None]
    mixed_local, y_total, conv_total, states = mamba_forward(
        ssm_x, bc_pre, gate_z, dt_raw, conv_w, head_rows, skip_row, conv_b
    )
    mixed_b = gather_seq(mixed_local, 1)
    mixed = mixed_b.astype(f32)
    scale_m = rms_factor(mixed)
    mamba_b = (mixed * scale_m * mamba_gain).astype(bf16)
    tokens_own = own_columns(tokens_b, cols).astype(f32)
    mamba_out = matmul(mamba_b, mamba_out_full)
    mid_own = tokens_own + matmul(attn_mix, attn_out_full) + mamba_out
    mid = gather_seq(mid_own.astype(bf16), 1).astype(f32)
    scale_two = rms_factor(mid)
    normed_two = mid * scale_two
    h2_b = (normed_two * gain_ffn).astype(bf16)
    both_pre = matmul(h2_b, ffn_full)
    gate_pre, up_pre = both_pre[:, :hidden_w], both_pre[:, hidden_w:]
    sigma = jax.nn.sigmoid(gate_pre)
    hidden_own = (gate_pre * sigma * up_pre).astype(bf16)

    cot_own = own_columns(cotangent, cols)
    d_hidden = reduce_seq(split(outer_cols(cot_own, down_full), 1))
    d_gate = (d_hidden * up_pre * (sigma * (1.0 + gate_pre * (1.0 - sigma)))).astype(bf16)
    d_up = (d_hidden * gate_pre * sigma).astype(bf16)
    d_both = jnp.concatenate([d_gate, d_up], axis=1)
    d_h2 = outer_cols(d_both, ffn_full)
    along = sum_over(jnp.mean(d_h2 * gain_ffn * normed_two, axis=1), ("seq",))
    g_gain_ffn = jnp.sum(d_h2 * normed_two, axis=0)
    d_h2_own = reduce_seq(split(d_h2, 1))
    d_mid = cot_own.astype(f32) + scale_two * (
        d_h2_own * own_columns(gain_ffn, cols)
        - mid_own * scale_two * along[:, None]
    )
    d_mid_b = d_mid.astype(bf16)
    hidden_b = gather_seq(hidden_own, 1)
    block_own = (mid_own + matmul(hidden_b, down_full)).astype(bf16)
    turned = swap_seq(split_rows(jnp.concatenate([block_own, d_mid_b], axis=1)))
    block_out = jnp.concatenate([t[:, :cols] for t in turned], axis=1)
    d_mid_rows = jnp.concatenate([t[:, cols:] for t in turned], axis=1)
    r_ffn = Reduction(inner_rows(h2_b, d_both))
    p_outs = jnp.concatenate(
        [
            inner_rows(left, right).reshape(groups, -1, cols)
            for left, right in (
                (attn_mix, d_mid_b),
                (mamba_b, d_mid_b),
                (hidden_b, cot_own),
            )
        ],
        axis=1,
    )
    r_outs = Reduction(p_outs.reshape(-1, cols))

    d_normed = reduce_seq(split(outer_cols(d_mid_b, mamba_out_full), 1))
    along_m = sum_over(jnp.sum(d_mid_b.astype(f32) * mamba_out, axis=1), ("seq",)) / (
        inner_all
    )
    d_attn = reduce_seq(split(outer_cols(d_mid_b, attn_out_full), 1)).astype(bf16)
    mixed_own = own_columns(mixed_b, inner).astype(f32)
    gain_own = own_columns(mamba_gain, inner)
    normed_own = mixed_own * scale_m
    g_mamba_gain = jnp.sum(d_normed * normed_own, axis=0)
    d_mixed = scale_m * (d_normed * gain_own - normed_own * along_m[:, None])
    r_ffn.advance(d_attn)
    d_queries, d_keys, d_values = attn_backward(
        queries, keys, values, lse, after(d_attn, (r_ffn.message, r_outs.message))
    )
    z_gate = jax.nn.sigmoid(gate_z)
    d_gate_z = (d_mixed * y_total * z_gate * (1.0 + gate_z * (1.0 - z_gate))).astype(bf16)
    d_early = jnp.concatenate([d_queries, d_gate_z], axis=1)
    r_early = Reduction(inner_rows(h1_b, d_early))
    r_ffn.advance(d_queries)
    r_outs.advance(d_queries)
    d_ssm_x, d_bc, d_dt_raw, g_conv, g_head = mamba_backward(
        d_mixed * gate_z * z_gate, conv_total, ssm_x, bc_pre, dt_raw, states, conv_w, head_rows,
        skip_row,
    )
    per_head_shards = HD // wide_k

    def shared_block(i):
        mine = kv_head == i // per_head_shards
        at = (i % per_head_shards) * wide_k
        return jnp.concatenate(
            [
                d_bc[:, i * wide_bc : (i + 1) * wide_bc],
                jnp.where(mine, d_keys[:, at : at + wide_k], 0.0),
                jnp.where(mine, d_values[:, at : at + wide_k], 0.0),
            ],
            axis=1,
        )

    r_outs.advance(d_dt_raw)
    d_shared, shared_message = reduce_seq_parts([shared_block(i) for i in range(shards)])
    d_shared = d_shared.astype(bf16)
    d_mid_in = jnp.concatenate([d_ssm_x, d_dt_raw], axis=1)
    r_early.advance(d_dt_raw)
    r_mid_in = Reduction(inner_rows(h1_b, after(d_mid_in, shared_message)))
    d_in = jnp.concatenate([d_early, d_mid_in, d_shared], axis=1)
    r_shared = Reduction(inner_rows(h1_b, d_shared))
    d_in = after(d_in, (r_early.message, r_mid_in.message, r_shared.message))
    d_h1, g_gain_mix = input_grad_parts(d_in, in_full, tokens_b, scale_one, 1)
    for _ in range(2):
        for chain in (r_mid_in, r_early, r_shared):
            chain.advance(d_h1)
    d_h1_own = reduce_seq(split(d_h1, 0))
    g_conv, g_head = after((g_conv, g_head), d_h1)
    every = slice(None)
    g_query, g_gate_z = r_early.finish([slice(None, wide_q), slice(wide_q, None)])
    g_ssm_x, g_ssm_dt = r_mid_in.finish([slice(None, inner), slice(inner, inner + heads)])
    g_ssm_bc, g_key, g_value = r_shared.finish(
        [slice(None, wide_bc), slice(wide_bc, wide_bc + wide_k), slice(wide_bc + wide_k, None)]
    )
    g_gate, g_up = r_ffn.finish([slice(None, hidden_w), slice(hidden_w, None)])
    (g_outs,) = r_outs.finish([every])
    g_attn_out, g_mamba_out = g_outs[:rows_a], g_outs[rows_a : rows_a + rows_m]
    g_down = g_outs[rows_a + rows_m :]
    x_own = block_in[0].astype(f32)
    scale_own = rms_factor(x_own)
    normed_x = x_own * scale_own
    d_norm = d_h1_own * gain_mix
    input_grad = d_mid_rows.astype(f32) + scale_own * (
        d_norm - normed_x * jnp.mean(d_norm * normed_x, axis=-1, keepdims=True)
    )

    width = inner_all + wide_bc * shards
    heads_all = HM
    own_heads = lax.dynamic_update_slice(
        jnp.zeros((3, heads_all), f32), g_head[:3, :heads], (0, place * heads)
    )
    line = jnp.concatenate(
        [g_gain_mix, own_heads.reshape(-1), jnp.zeros((width - model - 3 * heads_all,), f32)]
    )
    more = jnp.stack(
        [
            line,
            jnp.pad(g_gain_ffn, (0, width - model)),
            lax.dynamic_update_slice(jnp.zeros((width,), f32), g_mamba_gain, (place * inner,)),
        ]
    )
    small = jnp.pad(more, ((5, 0), (0, 0)))
    small = small + jnp.concatenate(
        [placed(g_conv[:, :inner], inner_all), g_conv[:, inner:]], axis=1
    )
    small = sum_over(small, ("seq", "dp"))
    line = small[5]

    def per_head(i):
        return line[model + i * heads_all : model + (i + 1) * heads_all]

    return (
        block_out[None],
        input_grad[None],
        line[:model],
        g_query,
        g_key,
        g_value,
        g_attn_out,
        g_gate_z,
        g_ssm_x,
        g_ssm_bc,
        g_ssm_dt,
        small[:KC],
        small[KC],
        per_head(0),
        per_head(1),
        per_head(2),
        small[7, :inner_all],
        g_mamba_out,
        small[6, :model],
        g_gate,
        g_up,
        g_down,
    )


def split_rows(array):
    return split(array, 0)


def solution(mesh):
    weight = P("dp", "seq")
    tokens = P("dp", "seq", None)
    args = (
        [tokens, tokens, P()]
        + [weight] * 8
        + [P()] * 6
        + [weight, P()]
        + [weight] * 3
    )
    outs = (
        [tokens, tokens, P()]
        + [weight] * 8
        + [P()] * 6
        + [weight, P()]
        + [weight] * 3
    )
    return jax.shard_map(
        per_device, mesh=mesh, in_specs=tuple(args), out_specs=tuple(outs), check_vma=False
    )
```

```python
import jax
import jax.numpy as jnp
from jax import lax
from jax.experimental import pallas as pl
from jax.experimental.pallas import tpu as pltpu
from jax.sharding import PartitionSpec as P

HQ = 8
HK = 2
HD = 64
HM = 24
PM = 64
NS = 128
KC = 4
CHUNK = 128

f32 = jnp.float32
bf16 = jnp.bfloat16
norm_eps = 1e-05
highest = lax.Precision.HIGHEST


def exchange(block, axis, step):
    return lax.ppermute(block, axis, [(i, i ^ step) for i in range(lax.axis_size(axis))])


def steps_of(axis):
    count, step, steps = lax.axis_size(axis), 1, []
    while step < count:
        steps.append(step)
        step *= 2
    return steps


def bit_of(axis, step):
    return (lax.axis_index(axis) & step) != 0


def reorder(blocks, axis):
    for step in steps_of(axis):
        flag = bit_of(axis, step)
        blocks = [jnp.where(flag, blocks[i ^ step], blocks[i]) for i in range(len(blocks))]
    return blocks


def spread(block, axis):
    found = {0: block}
    for step in reversed(steps_of(axis)):
        for offset in sorted(found):
            found[offset ^ step] = exchange(found[offset], axis, step)
    return [found[i] for i in range(len(found))]


def gather_seq(block, dim):
    return jnp.concatenate(reorder(spread(block, "seq"), "seq"), axis=dim)


def split(array, dim):
    count = lax.axis_size("seq")
    width = array.shape[dim] // count
    return [lax.slice_in_dim(array, i * width, (i + 1) * width, axis=dim) for i in range(count)]


def reduce_seq_parts(blocks):
    kept = dict(enumerate(reorder([b.astype(bf16) for b in blocks], "seq")))
    messages = []
    for step in steps_of("seq"):
        for offset in sorted(kept):
            if offset & step:
                messages.append(kept.pop(offset))
                got = exchange(messages[-1], "seq", step)
                kept[offset ^ step] = kept[offset ^ step].astype(f32) + got.astype(f32)
        kept = {k: (v.astype(bf16) if len(kept) > 1 else v) for k, v in kept.items()}
    return kept[0], messages


def reduce_seq(blocks):
    return reduce_seq_parts(blocks)[0]


def swap_seq(blocks):
    blocks = reorder(blocks, "seq")
    for step in reversed(steps_of("seq")):
        moved = [j for j in range(len(blocks)) if j & step]
        got = exchange(jnp.stack([blocks[j] for j in moved]), "seq", step)
        for i, j in enumerate(moved):
            blocks[j] = got[i]
    return reorder(blocks, "seq")


def sum_over(value, axes):
    for axis in axes:
        for step in steps_of(axis):
            value = value + exchange(value, axis, step)
    return value


def gather_dp(block):
    count, place = lax.axis_size("dp"), lax.axis_index("dp")
    parts = spread(block, "dp")
    whole = jnp.zeros((count,) + block.shape, block.dtype)
    for offset, part in enumerate(parts):
        whole = lax.dynamic_update_index_in_dim(whole, part, place ^ offset, 0)
    return whole


def after(value, gate):
    return value if gate is None else lax.optimization_barrier((value, gate))[0]


class Reduction:
    def __init__(self, grad):
        count = lax.axis_size("dp")
        self.left = steps_of("dp")
        self.send(grad.reshape(count, grad.shape[0] // count, grad.shape[1]))

    def send(self, held):
        step = self.left.pop(0)
        mine = bit_of("dp", step).astype(jnp.int32)
        pairs = held.reshape(held.shape[0] // 2, 2, held.shape[1], held.shape[2])
        self.message = lax.dynamic_index_in_dim(pairs, 1 - mine, 1, False).astype(bf16)
        self.stay = lax.dynamic_index_in_dim(pairs, mine, 1, False).astype(f32)
        self.got = exchange(self.message, "dp", step)

    def advance(self, gate=None):
        if self.left:
            self.send(self.stay + after(self.got, gate).astype(f32))
        return self.message

    def finish(self, cuts, gate=None):
        while self.left:
            self.advance()
        got = after(self.got, gate)[0].astype(f32)
        return [self.stay[0][:, c] + got[:, c] for c in cuts]


def matmul(left, right):
    return jnp.dot(left, right, preferred_element_type=f32)


def inner_rows(left, right):
    return lax.dot_general(left, right, (((0,), (0,)), ((), ())), preferred_element_type=f32)


def outer_cols(left, right):
    return lax.dot_general(left, right, (((1,), (1,)), ((), ())), preferred_element_type=f32)


def rms_factor(values):
    return lax.rsqrt(jnp.mean(values * values, axis=-1, keepdims=True) + norm_eps)


def masked_scores(q_ref, k_ref, at, first, count):
    scores = dot(q_ref[first : first + count, at], k_ref[0 : first + count, :], (1, 1)) * HD ** (-0.5)
    rows = lax.broadcasted_iota(jnp.int32, scores.shape, 0) + first
    cols = lax.broadcasted_iota(jnp.int32, scores.shape, 1)
    return jnp.where(cols <= rows, scores, -jnp.inf)


def attn_fwd_kernel(q_ref, k_ref, v_ref, mix_ref, lse_ref):
    length, width = q_ref.shape
    count = CHUNK if length % CHUNK == 0 else length
    for h in range(width // HD):
        at = slice(h * HD, (h + 1) * HD)
        for first in range(0, length, count):
            scores = masked_scores(q_ref, k_ref, at, first, count)
            top = jnp.max(scores, axis=1, keepdims=True)
            lse = top + jnp.log(jnp.sum(jnp.exp(scores - top), axis=1, keepdims=True))
            probs = jnp.exp(scores - lse).astype(bf16)
            here = slice(first, first + count)
            mix_ref[here, at] = dot(probs, v_ref[0 : first + count, :]).astype(bf16)
            lse_ref[here, h : h + 1] = lse


def attn_bwd_kernel(q_ref, k_ref, v_ref, lse_ref, grad_ref, dq_ref, dk_ref, dv_ref):
    length, width = q_ref.shape
    count = CHUNK if length % CHUNK == 0 else length
    dk_ref[...] = jnp.zeros_like(dk_ref)
    dv_ref[...] = jnp.zeros_like(dv_ref)
    for h in range(width // HD):
        at = slice(h * HD, (h + 1) * HD)
        for first in range(0, length, count):
            here, until = slice(first, first + count), slice(0, first + count)
            grad = grad_ref[here, at]
            probs = jnp.exp(masked_scores(q_ref, k_ref, at, first, count) - lse_ref[here, h : h + 1])
            dv_ref[until, :] = dv_ref[until, :] + dot(probs.astype(bf16), grad, (0, 0))
            d_probs = dot(grad, v_ref[until, :], (1, 1))
            inner = jnp.sum(probs * d_probs, axis=1, keepdims=True)
            d_scores = (probs * (d_probs - inner) * HD ** (-0.5)).astype(bf16)
            dq_ref[here, at] = dot(d_scores, k_ref[until, :]).astype(bf16)
            dk_ref[until, :] = dk_ref[until, :] + dot(d_scores, q_ref[here, at], (0, 0))


def input_grad_kernel(d_ref, w_ref, x_ref, scale_ref, out_ref, gain_ref):
    @pl.when(pl.program_id(0) == 0)
    def _():
        gain_ref[...] = jnp.zeros_like(gain_ref)

    grad = dot(d_ref[...], w_ref[...], (1, 1))
    out_ref[...] = grad.astype(bf16)
    normed = x_ref[...].astype(f32) * scale_ref[...]
    gain_ref[...] = gain_ref[...] + jnp.sum(grad * normed, axis=0, keepdims=True)


def input_grad_parts(d_in, weights, tokens, scale, blocks):
    length, width = d_in.shape
    model = weights.shape[0]
    count = length // blocks
    rows = lambda w: pl.BlockSpec((count, w), lambda i: (i, 0))
    grads, gain = pl.pallas_call(
        input_grad_kernel,
        grid=(blocks,),
        in_specs=[rows(width), full_spec(weights.shape), rows(model), rows(1)],
        out_specs=[rows(model), full_spec((1, model))],
        out_shape=[
            jax.ShapeDtypeStruct((length, model), bf16),
            jax.ShapeDtypeStruct((1, model), f32),
        ],
        name="input_grad",
    )(d_in, weights, tokens, scale)
    return grads, gain[0]


def attn_forward(queries, keys, values):
    length, width = queries.shape
    return pl.pallas_call(
        attn_fwd_kernel,
        out_shape=[
            jax.ShapeDtypeStruct((length, width), bf16),
            jax.ShapeDtypeStruct((length, 128), f32),
        ],
        name="attn_fwd",
    )(queries, keys, values)


def attn_backward(queries, keys, values, lse, grad_mix):
    return pl.pallas_call(
        attn_bwd_kernel,
        out_shape=[
            jax.ShapeDtypeStruct(queries.shape, bf16),
            jax.ShapeDtypeStruct(keys.shape, f32),
            jax.ShapeDtypeStruct(values.shape, f32),
        ],
        name="attn_bwd",
    )(queries, keys, values, lse, grad_mix)


def dot(left, right, over=(1, 0), precision=None):
    if left.dtype == f32 and precision is None:
        left_hi, right_hi = left.astype(bf16), right.astype(bf16)
        left_lo = (left - left_hi.astype(f32)).astype(bf16)
        right_lo = (right - right_hi.astype(f32)).astype(bf16)
        return (
            dot(left_hi, right_hi, over) + dot(left_hi, right_lo, over) + dot(left_lo, right_hi, over)
        )
    return lax.dot_general(
        left,
        right,
        (((over[0],), (over[1],)), ((), ())),
        precision=precision,
        preferred_element_type=f32,
    )


def head_map(lanes, inner):
    rows = lax.broadcasted_iota(jnp.int32, (lanes, inner), 0) * PM
    cols = lax.broadcasted_iota(jnp.int32, (lanes, inner), 1)
    return ((cols >= rows) & (cols < rows + PM)).astype(f32)


def chunk_terms(dt_in, log_rate, inner):
    count, lanes = dt_in.shape
    rows = lax.broadcasted_iota(jnp.int32, (count, count), 0)
    cols = lax.broadcasted_iota(jnp.int32, (count, count), 1)
    lower = rows >= cols
    dt = jax.nn.softplus(dt_in)
    rate = -jnp.exp(log_rate)
    cum = dot(lower.astype(f32), dt * rate, precision=highest)
    rest = jnp.exp(cum[count - 1 :, :] - cum)
    spread_map = head_map(lanes, inner)
    grown = dot(jnp.exp(cum), spread_map, precision=highest)
    tail = dot(rest * dt, spread_map, precision=highest)
    return lower, dt, rate, cum, rest, spread_map, grown, tail


def mamba_fwd_kernel(
    x_ref, bc_ref, z_ref, dt_ref, w_ref, bias_ref, head_ref, skip_ref,
    u_ref, y_ref, total_ref, state_ref, ext, state,
):
    count, inner = x_ref.shape

    @pl.when(pl.program_id(0) == 0)
    def _():
        state[...] = jnp.zeros_like(state)
        ext[...] = jnp.zeros_like(ext)

    ext[0:8, :] = ext[count : count + 8, :]
    ext[8 : 8 + count, :inner] = x_ref[...]
    ext[8 : 8 + count, inner:] = bc_ref[...].astype(f32)
    total = bias_ref[...] + w_ref[0:1, :] * ext[8 - KC + 1 : 8 - KC + 1 + count, :]
    for k in range(1, KC):
        total = total + w_ref[k : k + 1, :] * ext[8 - KC + 1 + k : 8 - KC + 1 + k + count, :]
    total_ref[...] = total
    act = total * jax.nn.sigmoid(total)
    x, b_rows, c_rows = act[:, :inner], act[:, inner : inner + NS], act[:, inner + NS :]
    lower, dt, rate, cum, rest, spread_map, grown, tail = chunk_terms(
        dt_ref[...] + head_ref[0:1, :], head_ref[1:2, :], inner
    )
    cum_t, dt_t = cum.T, dt.T
    x_b, b_b, c_b = x, b_rows, c_rows
    entering = state[...]
    state_ref[0] = entering
    between = dot(c_b, b_b, (1, 1))
    y_ref[...] = dot(c_b, entering) * grown + skip_ref[...] * x
    for h in range(inner // PM):
        at = slice(h * PM, (h + 1) * PM)
        gap = jnp.where(lower, cum[:, h : h + 1] - cum_t[h : h + 1, :], 0.0)
        mix = jnp.where(lower, jnp.exp(gap) * between * dt_t[h : h + 1, :], 0.0)
        y_ref[:, at] = y_ref[:, at] + dot(mix, x_b[:, at])
    state[...] = entering * grown[count - 1 :, :] + dot(b_b, (x * tail), (0, 0))
    z = z_ref[...]
    u_ref[...] = (y_ref[...] * (z * jax.nn.sigmoid(z))).astype(bf16)


def mamba_bwd_kernel(
    dy_ref, total_ref, x_ref, bc_ref, dt_ref, state_ref, w_ref, head_ref, skip_ref,
    dx_ref, dbc_ref, ddt_ref, gconv_ref, ghead_ref, ext, carry, rows_ref, dact,
):
    count, inner = x_ref.shape
    lanes = dt_ref.shape[1]

    @pl.when(pl.program_id(0) == 0)
    def _():
        carry[...] = jnp.zeros_like(carry)
        ext[...] = jnp.zeros_like(ext)
        rows_ref[...] = jnp.zeros_like(rows_ref)
        gconv_ref[...] = jnp.zeros_like(gconv_ref)
        ghead_ref[...] = jnp.zeros_like(ghead_ref)

    total = total_ref[...]
    gate = jax.nn.sigmoid(total)
    act = total * gate
    x, b_rows, c_rows = act[:, :inner], act[:, inner : inner + NS], act[:, inner + NS :]
    dy = dy_ref[...]
    skipped = jnp.sum(dy * x, axis=0, keepdims=True)
    dt_in = dt_ref[...] + head_ref[0:1, :]
    lower, dt, rate, cum, rest, spread_map, grown, tail = chunk_terms(
        dt_in, head_ref[1:2, :], inner
    )
    cum_t, dt_t = cum.T, dt.T
    x_b, b_b, c_b, dy_b = x, b_rows, c_rows, dy
    entering, leaving = state_ref[0], carry[...]
    entering_b, leaving_b = entering, leaving
    last = grown[count - 1 :, :]
    dye_b = (dy * grown)
    y_state = dot(c_b, entering_b) * grown
    d_xw = dot(b_b, leaving_b)
    d_b = dot((x * tail), leaving_b, (1, 1))
    d_c = dot(dye_b, entering_b, (1, 1))
    carry[...] = leaving * last + dot(c_b, dye_b, (0, 0))
    d_cum = dot(dy * y_state, spread_map, (1, 1), highest)
    d_tail = dot(d_xw * x, spread_map, (1, 1), highest)
    d_last = dot(
        jnp.sum(leaving * entering, axis=0, keepdims=True) * last, spread_map, (1, 1), highest
    )
    dact[:, :inner] = skip_ref[...] * dy + d_xw * tail
    between = dot(c_b, b_b, (1, 1))
    d_between = jnp.zeros_like(between)
    lane = lax.broadcasted_iota(jnp.int32, (count, lanes), 1)
    for h in range(inner // PM):
        at = slice(h * PM, (h + 1) * PM)
        gap = jnp.where(lower, cum[:, h : h + 1] - cum_t[h : h + 1, :], 0.0)
        decay = jnp.where(lower, jnp.exp(gap), 0.0)
        d_mix = dot(dy_b[:, at], x_b[:, at], (1, 1)) * decay
        d_between = d_between + d_mix * dt_t[h : h + 1, :]
        part = d_mix * between
        rows_ref[h : h + 1, :] = jnp.sum(part, axis=0, keepdims=True)
        along = jnp.sum(part * dt_t[h : h + 1, :], axis=1, keepdims=True)
        d_cum = d_cum + jnp.where(lane == h, along, 0.0)
        mix = (decay * between * dt_t[h : h + 1, :])
        dact[:, at] = dact[:, at] + dot(mix, dy_b[:, at], (0, 0))
    d_between_b = d_between
    d_c = d_c + dot(d_between_b, b_b)
    d_b = d_b + dot(d_between_b, c_b, (0, 0))
    dact[:, inner : inner + NS] = d_b
    dact[:, inner + NS :] = d_c
    d_dt = rows_ref[...].T
    d_decay = d_tail * rest * dt
    d_cum = d_cum - d_decay - dt * d_dt
    d_last = d_last + jnp.sum(d_decay, axis=0, keepdims=True)
    d_step = dot(lower.astype(f32), d_cum, (0, 0), highest) + d_last
    d_dt = d_dt + d_tail * rest + d_step * rate
    d_raw = d_dt * jax.nn.sigmoid(dt_in)
    ddt_ref[...] = d_raw.astype(bf16)
    ghead_ref[0:1, :] = ghead_ref[0:1, :] + jnp.sum(d_raw, axis=0, keepdims=True)
    ghead_ref[1:2, :] = ghead_ref[1:2, :] + jnp.sum(d_step * dt, axis=0, keepdims=True) * rate
    ghead_ref[2:3, :] = ghead_ref[2:3, :] + dot(skipped, spread_map, (1, 1), highest)
    d_total = dact[...] * (gate * (1.0 + total * (1.0 - gate)))
    ext[count : count + 8, :] = ext[0:8, :]
    ext[0:count, :] = d_total
    gconv_ref[KC : KC + 1, :] = gconv_ref[KC : KC + 1, :] + jnp.sum(d_total, axis=0, keepdims=True)
    d_x, d_bc = jnp.zeros_like(x), jnp.zeros((count, 2 * NS), f32)
    x_in, bc_in = x_ref[...], bc_ref[...].astype(f32)
    for k in range(KC):
        moved = ext[KC - 1 - k : KC - 1 - k + count, :]
        d_x = d_x + w_ref[k : k + 1, :inner] * moved[:, :inner]
        d_bc = d_bc + w_ref[k : k + 1, inner:] * moved[:, inner:]
        gconv_ref[k : k + 1, :inner] = gconv_ref[k : k + 1, :inner] + jnp.sum(
            x_in * moved[:, :inner], axis=0, keepdims=True
        )
        gconv_ref[k : k + 1, inner:] = gconv_ref[k : k + 1, inner:] + jnp.sum(
            bc_in * moved[:, inner:], axis=0, keepdims=True
        )
    dx_ref[...] = d_x.astype(bf16)
    dbc_ref[...] = d_bc


def rows_spec(width, chunk, chunks, back):
    return pl.BlockSpec((chunk, width), lambda c: (chunks - 1 - c if back else c, 0))


def full_spec(shape):
    return pl.BlockSpec(shape, lambda c: (0,) * len(shape))


def mamba_forward(x_pre, bc_pre, gate_z, dt_raw, conv_w, head_rows, skip_row, conv_b):
    length, inner = x_pre.shape
    chunk = CHUNK if length % CHUNK == 0 else length
    chunks = length // chunk
    wide = inner + 2 * NS
    rows = lambda width: rows_spec(width, chunk, chunks, False)
    return pl.pallas_call(
        mamba_fwd_kernel,
        grid=(chunks,),
        in_specs=[
            rows(inner), rows(2 * NS), rows(inner), rows(dt_raw.shape[1]),
            full_spec(conv_w.shape), full_spec(conv_b.shape), full_spec(head_rows.shape),
            full_spec(skip_row.shape),
        ],
        out_specs=[
            rows(inner), rows(inner), rows(wide),
            pl.BlockSpec((1, NS, inner), lambda c: (c, 0, 0)),
        ],
        out_shape=[
            jax.ShapeDtypeStruct((length, inner), bf16),
            jax.ShapeDtypeStruct((length, inner), f32),
            jax.ShapeDtypeStruct((length, wide), f32),
            jax.ShapeDtypeStruct((chunks, NS, inner), f32),
        ],
        scratch_shapes=[pltpu.VMEM((chunk + 8, wide), f32), pltpu.VMEM((NS, inner), f32)],
        name="mamba_fwd",
    )(x_pre, bc_pre, gate_z, dt_raw, conv_w, conv_b, head_rows, skip_row)


def mamba_backward(
    d_y, total, x_pre, bc_pre, dt_raw, states, conv_w, head_rows, skip_row
):
    length, inner = x_pre.shape
    chunks = states.shape[0]
    chunk = length // chunks
    wide, lanes = inner + 2 * NS, dt_raw.shape[1]
    rows = lambda width: rows_spec(width, chunk, chunks, True)
    return pl.pallas_call(
        mamba_bwd_kernel,
        grid=(chunks,),
        in_specs=[
            rows(inner), rows(wide), rows(inner), rows(2 * NS), rows(lanes),
            pl.BlockSpec((1, NS, inner), lambda c: (chunks - 1 - c, 0, 0)),
            full_spec(conv_w.shape), full_spec(head_rows.shape), full_spec(skip_row.shape),
        ],
        out_specs=[
            rows(inner), rows(2 * NS), rows(lanes),
            full_spec((8, wide)), full_spec((8, lanes)),
        ],
        out_shape=[
            jax.ShapeDtypeStruct((length, inner), bf16),
            jax.ShapeDtypeStruct((length, 2 * NS), f32),
            jax.ShapeDtypeStruct((length, lanes), bf16),
            jax.ShapeDtypeStruct((8, wide), f32),
            jax.ShapeDtypeStruct((8, lanes), f32),
        ],
        scratch_shapes=[
            pltpu.VMEM((chunk + 8, wide), f32),
            pltpu.VMEM((NS, inner), f32),
            pltpu.VMEM((lanes, chunk), f32),
            pltpu.VMEM((chunk, wide), f32),
        ],
        name="mamba_bwd",
    )(d_y, total, x_pre, bc_pre, dt_raw, states, conv_w, head_rows, skip_row)


def own_columns(array, width):
    return lax.dynamic_slice_in_dim(array, lax.axis_index("seq") * width, width, array.ndim - 1)


def placed(array, width):
    start = [0] * (array.ndim - 1) + [lax.axis_index("seq") * array.shape[-1]]
    return lax.dynamic_update_slice(
        jnp.zeros(array.shape[:-1] + (width,), array.dtype), array, start
    )


def per_device(
    block_in,
    out_grad,
    gain_mix,
    w_query,
    w_key,
    w_value,
    w_attn_out,
    w_gate_z,
    w_ssm_x,
    w_ssm_bc,
    w_ssm_dt,
    conv_weight,
    conv_bias,
    dt_bias,
    a_log,
    skip_d,
    mamba_gain,
    w_mamba_out,
    gain_ffn,
    w_gate,
    w_up,
    w_down,
):
    shards = lax.axis_size("seq")
    place = lax.axis_index("seq")
    groups = lax.axis_size("dp")
    model = block_in.shape[2]
    wide_q, wide_k, wide_bc = w_query.shape[1], w_key.shape[1], w_ssm_bc.shape[1]
    inner, heads, hidden_w = w_gate_z.shape[1], w_ssm_dt.shape[1], w_gate.shape[1]
    cols = w_attn_out.shape[1]
    kv_head = (place * (wide_q // HD)) // (HQ // HK)

    lanes = 128
    fill = -heads % lanes
    pack_in = jnp.concatenate(
        [w_query, w_gate_z, w_ssm_x, jnp.pad(w_ssm_dt, ((0, 0), (0, fill))), w_ssm_bc, w_key, w_value],
        axis=1,
    )
    in_full = gather_dp(pack_in).reshape(model, -1)
    out_grad_b, block_in_b = out_grad[0], block_in[0]
    token_blocks = spread(jnp.concatenate([block_in_b, out_grad_b], axis=1), "seq")
    rows_a, rows_m = w_attn_out.shape[0], w_mamba_out.shape[0]
    pack_out = jnp.concatenate([w_attn_out, w_mamba_out, w_down], axis=0)
    rows_w = w_gate.shape[0]
    stacks = pack_out.shape[0] // rows_w
    pack_rest = jnp.concatenate(
        [w_gate, w_up] + [pack_out[i * rows_w : (i + 1) * rows_w] for i in range(stacks)], axis=1
    )
    rest_full = lax.all_gather(pack_rest, "dp", axis=0)
    ffn_full = rest_full[:, :, : 2 * hidden_w].reshape(model, 2 * hidden_w)
    out_full = jnp.concatenate(
        [
            rest_full[:, :, 2 * hidden_w + i * cols : 2 * hidden_w + (i + 1) * cols]
            for i in range(stacks)
        ],
        axis=1,
    )
    attn_out_full = out_full[:, :rows_a].reshape(-1, cols)
    mamba_out_full = out_full[:, rows_a : rows_a + rows_m].reshape(-1, cols)
    down_full = out_full[:, rows_a + rows_m :].reshape(-1, cols)

    both = jnp.concatenate(reorder(token_blocks, "seq"), axis=0)
    tokens_b, cotangent = both[:, :model], both[:, model:]
    tokens = tokens_b.astype(f32)
    row_count = tokens.shape[0]
    local_rows = block_in.shape[1]
    scale_one = rms_factor(tokens)
    h1_b = (tokens * scale_one * gain_mix).astype(bf16)
    cuts = [wide_q, inner, inner, heads + fill, wide_bc + 2 * wide_k]
    edges = [sum(cuts[:i]) for i in range(len(cuts) + 1)]
    shared = matmul(h1_b, in_full[:, edges[4] :])
    shared_all = reorder(spread(shared, "seq"), "seq")
    queries = matmul(h1_b, in_full[:, : edges[1]]).astype(bf16)
    gate_z = matmul(h1_b, in_full[:, edges[1] : edges[2]])
    ssm_x = matmul(h1_b, in_full[:, edges[2] : edges[3]])
    dt_raw = matmul(h1_b, in_full[:, edges[3] : edges[4]])
    bc_pre = jnp.concatenate([s[:, :wide_bc] for s in shared_all], axis=1)
    keys_all = jnp.concatenate([s[:, wide_bc : wide_bc + wide_k] for s in shared_all], axis=1)
    values_all = jnp.concatenate([s[:, wide_bc + wide_k :] for s in shared_all], axis=1)
    keys = lax.dynamic_slice_in_dim(keys_all.astype(bf16), kv_head * HD, HD, 1)
    values = lax.dynamic_slice_in_dim(values_all.astype(bf16), kv_head * HD, HD, 1)

    attn_local, lse = attn_forward(queries, keys, values)
    attn_mix = gather_seq(attn_local, 1)

    inner_all = inner * shards

    def own_conv(array):
        return jnp.concatenate(
            [own_columns(array[..., :inner_all], inner), array[..., inner_all:]], axis=-1
        )

    conv_w, conv_b = own_conv(conv_weight), own_conv(conv_bias)[None]
    head_rows = jnp.pad(
        jnp.stack([own_columns(dt_bias, heads), own_columns(a_log, heads)]), ((0, 0), (0, fill))
    )
    skip_row = jnp.repeat(own_columns(skip_d, heads), inner // heads)[None]
    mixed_local, y_total, conv_total, states = mamba_forward(
        ssm_x, bc_pre, gate_z, dt_raw, conv_w, head_rows, skip_row, conv_b
    )
    mixed_b = gather_seq(mixed_local, 1)
    cot_own = own_columns(cotangent, cols)
    d_hidden, hidden_messages = reduce_seq_parts(split(outer_cols(cot_own, down_full), 1))
    mixed = mixed_b.astype(f32)
    scale_m = rms_factor(mixed)
    mamba_b = (mixed * scale_m * mamba_gain).astype(bf16)
    tokens_own = own_columns(tokens_b, cols).astype(f32)
    mamba_b = after(mamba_b, hidden_messages[:-1])
    mamba_out = matmul(mamba_b, mamba_out_full)
    mid_own = tokens_own + matmul(attn_mix, attn_out_full) + mamba_out
    mid = gather_seq(mid_own.astype(bf16), 1).astype(f32)
    scale_two = rms_factor(mid)
    normed_two = mid * scale_two
    h2_b = (normed_two * gain_ffn).astype(bf16)
    both_pre = matmul(h2_b, ffn_full)
    gate_pre, up_pre = both_pre[:, :hidden_w], both_pre[:, hidden_w:]
    sigma = jax.nn.sigmoid(gate_pre)
    hidden_own = (gate_pre * sigma * up_pre).astype(bf16)

    d_gate = (d_hidden * up_pre * (sigma * (1.0 + gate_pre * (1.0 - sigma)))).astype(bf16)
    d_up = (d_hidden * gate_pre * sigma).astype(bf16)
    d_both = jnp.concatenate([d_gate, d_up], axis=1)
    d_h2 = outer_cols(d_both, ffn_full)
    along = sum_over(jnp.mean(d_h2 * gain_ffn * normed_two, axis=1), ("seq",))
    g_gain_ffn = jnp.sum(d_h2 * normed_two, axis=0)
    d_h2_own = reduce_seq(split(d_h2, 1))
    d_mid = cot_own.astype(f32) + scale_two * (
        d_h2_own * own_columns(gain_ffn, cols)
        - mid_own * scale_two * along[:, None]
    )
    d_mid_b = d_mid.astype(bf16)
    hidden_b = gather_seq(hidden_own, 1)
    block_own = (mid_own + matmul(hidden_b, down_full)).astype(bf16)
    turned = swap_seq(split_rows(jnp.concatenate([block_own, d_mid_b], axis=1)))
    block_out = jnp.concatenate([t[:, :cols] for t in turned], axis=1)
    d_mid_rows = jnp.concatenate([t[:, cols:] for t in turned], axis=1)
    r_ffn = Reduction(inner_rows(h2_b, d_both))
    p_outs = jnp.concatenate(
        [
            inner_rows(left, right).reshape(groups, -1, cols)
            for left, right in (
                (attn_mix, d_mid_b),
                (mamba_b, d_mid_b),
                (hidden_b, cot_own),
            )
        ],
        axis=1,
    )
    r_outs = Reduction(p_outs.reshape(-1, cols))

    d_normed = reduce_seq(split(outer_cols(d_mid_b, mamba_out_full), 1))
    along_m = sum_over(jnp.sum(d_mid_b.astype(f32) * mamba_out, axis=1), ("seq",)) / (
        inner_all
    )
    d_attn = reduce_seq(split(outer_cols(d_mid_b, attn_out_full), 1)).astype(bf16)
    mixed_own = own_columns(mixed_b, inner).astype(f32)
    gain_own = own_columns(mamba_gain, inner)
    normed_own = mixed_own * scale_m
    g_mamba_gain = jnp.sum(d_normed * normed_own, axis=0)
    d_mixed = scale_m * (d_normed * gain_own - normed_own * along_m[:, None])
    r_ffn.advance(d_attn)
    d_queries, d_keys, d_values = attn_backward(
        queries, keys, values, lse, after(d_attn, (r_ffn.message, r_outs.message))
    )
    z_gate = jax.nn.sigmoid(gate_z)
    d_gate_z = (d_mixed * y_total * z_gate * (1.0 + gate_z * (1.0 - z_gate))).astype(bf16)
    d_early = jnp.concatenate([d_queries, d_gate_z], axis=1)
    r_early = Reduction(inner_rows(h1_b, d_early))
    r_ffn.advance(d_queries)
    d_ssm_x, d_bc, d_dt_raw, g_conv, g_head = mamba_backward(
        after(d_mixed * gate_z * z_gate, (r_ffn.message, r_early.message)), conv_total, ssm_x, bc_pre, dt_raw, states, conv_w, head_rows,
        skip_row,
    )
    per_head_shards = HD // wide_k

    def shared_block(i):
        mine = kv_head == i // per_head_shards
        at = (i % per_head_shards) * wide_k
        return jnp.concatenate(
            [
                d_bc[:, i * wide_bc : (i + 1) * wide_bc],
                jnp.where(mine, d_keys[:, at : at + wide_k], 0.0),
                jnp.where(mine, d_values[:, at : at + wide_k], 0.0),
            ],
            axis=1,
        )

    r_outs.advance(d_dt_raw)
    d_shared, shared_messages = reduce_seq_parts([shared_block(i) for i in range(shards)])
    d_shared = d_shared.astype(bf16)
    d_mid_in = jnp.concatenate([d_ssm_x, d_dt_raw], axis=1)
    r_early.advance(d_dt_raw)
    r_mid_in = Reduction(inner_rows(h1_b, after(d_mid_in, (shared_messages[-1], r_outs.message))))
    d_in = jnp.concatenate([d_early, d_mid_in, d_shared], axis=1)
    r_shared = Reduction(inner_rows(h1_b, d_shared))
    r_outs.advance(d_mid_in)
    d_in = after(d_in, (r_early.message, r_mid_in.message, r_shared.message, r_outs.message))
    d_h1, g_gain_mix = input_grad_parts(d_in, in_full, tokens_b, scale_one, 1)
    for chain in (r_mid_in, r_early, r_shared):
        chain.advance(d_h1)
    d_h1_own, h1_messages = reduce_seq_parts(split(d_h1, 0))
    g_conv, g_head = after((g_conv, g_head), d_h1)
    for chain in (r_mid_in, r_early, r_shared):
        chain.advance(h1_messages[-1])
    every = slice(None)
    g_query, g_gate_z = r_early.finish([slice(None, wide_q), slice(wide_q, None)])
    g_ssm_x, g_ssm_dt = r_mid_in.finish([slice(None, inner), slice(inner, inner + heads)])
    g_ssm_bc, g_key, g_value = r_shared.finish(
        [slice(None, wide_bc), slice(wide_bc, wide_bc + wide_k), slice(wide_bc + wide_k, None)]
    )
    g_gate, g_up = r_ffn.finish([slice(None, hidden_w), slice(hidden_w, None)], d_h1)
    (g_outs,) = r_outs.finish([every], d_h1)
    g_attn_out, g_mamba_out = g_outs[:rows_a], g_outs[rows_a : rows_a + rows_m]
    g_down = g_outs[rows_a + rows_m :]
    x_own = block_in[0].astype(f32)
    scale_own = rms_factor(x_own)
    normed_x = x_own * scale_own
    d_norm = d_h1_own * gain_mix
    input_grad = d_mid_rows.astype(f32) + scale_own * (
        d_norm - normed_x * jnp.mean(d_norm * normed_x, axis=-1, keepdims=True)
    )

    width = inner_all + wide_bc * shards
    heads_all = HM
    own_heads = lax.dynamic_update_slice(
        jnp.zeros((3, heads_all), f32), g_head[:3, :heads], (0, place * heads)
    )
    line = jnp.concatenate(
        [g_gain_mix, own_heads.reshape(-1), jnp.zeros((width - model - 3 * heads_all,), f32)]
    )
    more = jnp.stack(
        [
            line,
            jnp.pad(g_gain_ffn, (0, width - model)),
            lax.dynamic_update_slice(jnp.zeros((width,), f32), g_mamba_gain, (place * inner,)),
        ]
    )
    small = jnp.pad(more, ((5, 0), (0, 0)))
    small = small + jnp.concatenate(
        [placed(g_conv[:, :inner], inner_all), g_conv[:, inner:]], axis=1
    )
    small = sum_over(small, ("seq", "dp"))
    line = small[5]

    def per_head(i):
        return line[model + i * heads_all : model + (i + 1) * heads_all]

    return (
        block_out[None],
        input_grad[None],
        line[:model],
        g_query,
        g_key,
        g_value,
        g_attn_out,
        g_gate_z,
        g_ssm_x,
        g_ssm_bc,
        g_ssm_dt,
        small[:KC],
        small[KC],
        per_head(0),
        per_head(1),
        per_head(2),
        small[7, :inner_all],
        g_mamba_out,
        small[6, :model],
        g_gate,
        g_up,
        g_down,
    )


def split_rows(array):
    return split(array, 0)


def solution(mesh):
    weight = P("dp", "seq")
    tokens = P("dp", "seq", None)
    args = (
        [tokens, tokens, P()]
        + [weight] * 8
        + [P()] * 6
        + [weight, P()]
        + [weight] * 3
    )
    outs = (
        [tokens, tokens, P()]
        + [weight] * 8
        + [P()] * 6
        + [weight, P()]
        + [weight] * 3
    )
    return jax.shard_map(
        per_device, mesh=mesh, in_specs=tuple(args), out_specs=tuple(outs), check_vma=False
    )
```
